128 devices in a mesh: row: 16 (over z, x), col: 8 (over y, core).
Axes of the slice: x: 4, y: 4, z: 4, core: 2. Of those that a mesh axis runs over, the one named last changes fastest.
Arguments:
- factor: float32 [16384, 16384], P('row', 'col'), may hold values from -0.24 to 0.24
- adjoint: float32 [16384, 16384], P('row', 'col'), may hold values from -6 to 6
- inverse: float32 [2, 256, 256], replicated, may hold values from -1 to 3, as said below
Outputs:
- adjoint_out: float32 [16384, 16384], P('row', 'col')
The draws below stay inside these ranges and needn't reach their ends.
Inputs may be any that keep to these rules, and one draw needn't show every extreme that they name: Each inverse[j] is lower triangular, with every diagonal entry larger than the sum of the magnitudes of the other entries of its row.
All inputs are finite; a program needn't handle non-finite values.
Results may differ from the reference program's by a relative error of at most 0.00011.
Values sent between devices are 32-bit elements; how exact they have to be, the bound alone decides.
No kernel may reach another device: no remote copies, remote signals or barrier semaphores. Data moves between devices by JAX's collectives and lax.ppermute only.
A program may use at most 128 MiB of HBM per device.

```python
import jax
import jax.numpy as jnp
from jax import lax

NB = 256
TPR = 4
TPC = 8
NT = 64
N = 16384
N_ROW = 16
N_COL = 8


def draw_inverse(key, part):
    key_off, key_diag = jax.random.split(key)
    off_part = jax.random.uniform(key_off, (2, NB, NB), jnp.float32, -1.0, 1.0) * (1.2 / NB)
    diag_part = jax.random.uniform(key_diag, (2, NB), jnp.float32, 1.0, 2.0)
    strict_lower = jnp.tril(off_part, -1)
    return strict_lower + diag_part[:, :, None] * jnp.eye(NB, dtype=jnp.float32)


def shard_levels(stream_key, extent, shards, smallest, top_value):
    gain, own = 1.0, jax.random.fold_in(stream_key, 6)
    for dim, parts in shards:
        draws = jnp.exp(jax.random.uniform(jax.random.fold_in(own, dim), (parts,), jnp.float32, smallest / len(shards), top_value / len(shards)))
        gain = gain * jnp.repeat(draws, extent[dim] // parts).reshape([-1 if axis == dim else 1 for axis in range(len(extent))])
    return gain


def normal_values(rng, shape, width, reach, cuts=(), kind=jnp.bfloat16):
    values = jax.random.normal(rng, shape, jnp.float32) * width
    if len(cuts) > 0:
        values = shard_levels(rng, shape, cuts, -0.22, 0.18) * values
    return jnp.clip(values, min=-reach, max=reach).astype(kind)


def setup_inputs(seed: int = 0) -> dict:
    streams_of = jax.random.split(jax.random.key(seed), 4)
    factor = normal_values(streams_of[0], (N, N), 0.04, 0.24, ((0, 16), (1, 8)), jnp.float32)
    adjoint = normal_values(streams_of[1], (N, N), 1.0, 6.0, ((0, 16), (1, 8)), jnp.float32)
    inverse = draw_inverse(jax.random.fold_in(streams_of[3], 71), 0)
    return dict(factor=factor, adjoint=adjoint, inverse=inverse)


def matmul_high(left, right):
    return jnp.dot(left.astype(jnp.float32), right.astype(jnp.float32), precision=lax.Precision.HIGHEST, preferred_element_type=jnp.float32)

def halved_lower(matrix):
    return jnp.tril(matrix) - 0.5 * jnp.diag(jnp.diagonal(matrix))

def to_global(stored):
    blocks = stored.reshape(N_ROW, TPR, NB, N_COL, TPC, NB).transpose(1, 0, 2, 4, 3, 5)
    return blocks.reshape(NT * NB, NT * NB)

def to_stored(matrix):
    blocks = matrix.reshape(TPR, N_ROW, NB, TPC, N_COL, NB).transpose(1, 0, 2, 4, 3, 5)
    return blocks.reshape(NT * NB, NT * NB)

def reference(factor, adjoint, inverse):
    full_factor = to_global(factor)
    grad = to_global(adjoint)
    identity = jnp.eye(NB, dtype=jnp.float32)
    for position, panel_tile in enumerate((NT // 2, NT // 2 - 1)):
        start = panel_tile * NB
        finish = start + NB
        inverse_tile = inverse[position]
        factor_diag = lax.linalg.triangular_solve(inverse_tile, identity, left_side=True, lower=True)
        offdiag = matmul_high(grad[finish:, start:finish], inverse_tile)
        factor_row = full_factor[start:finish, :start]
        new_trailing = grad[finish:, :start] - matmul_high(offdiag, factor_row)
        dprime = jnp.tril(grad[start:finish, start:finish] - matmul_high(offdiag.T, full_factor[finish:, start:finish]))
        wmat = matmul_high(matmul_high(inverse_tile.T, halved_lower(matmul_high(factor_diag.T, dprime))), inverse_tile)
        sym = wmat + wmat.T
        new_row = grad[start:finish, :start] - matmul_high(offdiag.T, full_factor[finish:, :start]) - matmul_high(sym, factor_row)
        grad = grad.at[finish:, :start].set(new_trailing)
        grad = grad.at[start:finish, :start].set(new_row)
        grad = grad.at[finish:, start:finish].set(offdiag)
        grad = grad.at[start:finish, start:finish].set(halved_lower(sym))
    return to_stored(grad)
```

```python
import jax
import jax.numpy as jnp
from jax import lax
from jax.sharding import Mesh
from jax.sharding import PartitionSpec as P

ROW = ("z", "x")
COL = ("y", "core")


def product(left, right):
    return jnp.dot(left, right, precision=lax.Precision.HIGHEST, preferred_element_type=jnp.float32)


def product_t(left, right):
    return lax.dot_general(
        left,
        right,
        (((0,), (0,)), ((), ())),
        precision=lax.Precision.HIGHEST,
        preferred_element_type=jnp.float32,
    )


def masks(width):
    rows = lax.broadcasted_iota(jnp.int32, (width, width), 0)
    cols = lax.broadcasted_iota(jnp.int32, (width, width), 1)
    return rows > cols, rows == cols


def tril(matrix):
    below, diag = masks(matrix.shape[0])
    return jnp.where(below | diag, matrix, 0.0)


def halved_lower(matrix):
    below, diag = masks(matrix.shape[0])
    return jnp.where(below, matrix, jnp.where(diag, 0.5 * matrix, 0.0))


def lower_inverse(tile):
    width = tile.shape[0]
    below, diag = masks(width)
    scale = 1.0 / jnp.sum(jnp.where(diag, tile, 0.0), axis=1, keepdims=True)
    scale_row = 1.0 / jnp.sum(jnp.where(diag, tile, 0.0), axis=0, keepdims=True)
    power = jnp.where(below, tile * scale, 0.0)
    eye = diag.astype(jnp.float32)
    total = eye - power
    reach = 2
    while reach < width:
        power = product(power, power)
        total = total + product(total, power)
        reach *= 2
    return total * scale_row


def adjoint_diag(inverse_tile, factor_diag, dprime):
    wmat = product(
        product_t(inverse_tile, halved_lower(product_t(factor_diag, tril(dprime)))), inverse_tile
    )
    return wmat + wmat.T


def column_broadcast(block):
    rows, width = block.shape
    y = lax.axis_index("y")
    core = lax.axis_index("core")
    ny = lax.axis_size("y")
    half = rows // 2
    halves = block.reshape(2, half, width)
    mine = jnp.where(core == 0, halves[0], halves[1])
    other = jnp.where(core == 0, halves[1], halves[0])
    received = lax.ppermute(other, "core", [(0, 1), (1, 0)])
    has = ((y == 0) & (core == 0)) | ((y != 0) & (core == 1))
    sent = jnp.where(has, mine, received)
    piece = half // ny
    scattered = lax.all_to_all(sent.reshape(ny, piece, width), "y", 0, 0)
    pair = jnp.stack([scattered[0], scattered[ny - 1]])
    spread = jnp.broadcast_to(pair[None], (ny, 2, piece, width))
    gathered = lax.all_to_all(spread, "y", 0, 0)
    own = gathered.transpose(1, 0, 2, 3).reshape(2, half, width)
    theirs = lax.ppermute(own, "core", [(0, 1), (1, 0)])
    top = jnp.where(core == 0, own, theirs)
    bottom = jnp.where(core == 0, theirs, own)
    return jnp.concatenate([top, bottom], axis=1)


def per_device(factor, adjoint, inverse):
    w = inverse.shape[-1]
    rows = lax.axis_size("z") * lax.axis_size("x")
    p = lax.axis_index(ROW)
    q = lax.axis_index(COL)
    last_p, last_q = rows - 1, lax.axis_size(COL) - 1
    low, left = 2 * w, 4 * w
    inv0, inv1 = inverse[0], inverse[1]

    row_sent = jnp.where(p == 0, factor[low : low + w, :left], factor[w:low, :left])
    piece = w // rows
    got = lax.all_to_all(row_sent.reshape(rows, piece, left), ROW, 0, 0)
    pair = jnp.stack([got[0], got[rows - 1]])
    both = lax.all_gather(pair, ROW, axis=0)
    factor_rows = both.transpose(1, 0, 2, 3).reshape(2 * w, left)
    r0, r1 = factor_rows[:w], factor_rows[w:]

    first = q == 0
    adj_col = jnp.where(first, adjoint[low:, left : left + w], adjoint[low:, left - w : left])
    fac_col = jnp.where(first, factor[low:, left : left + w], factor[low:, left - w : left])
    diag31 = adjoint[w:low, left - w : left]
    extra = jnp.concatenate([diag31[: w // 2], diag31[w // 2 :]], axis=1)
    block = jnp.concatenate([jnp.concatenate([adj_col, fac_col], axis=1), extra], axis=0)
    panels = column_broadcast(block)
    l0, c0 = panels[0, :low, :w], panels[0, :low, w:]
    l1, c1 = panels[1, :low, :w], panels[1, :low, w:]
    diag31 = jnp.concatenate([panels[1, low:, :w], panels[1, low:, w:]], axis=0)
    at_first = p == 0
    skip = at_first & (lax.broadcasted_iota(jnp.int32, (low, w), 0) < w)
    raw_diag = jnp.where(at_first, l0[:w], 0.0)
    raw_next = jnp.where(at_first, l1[:w], 0.0)
    raw_r31 = jnp.where(at_first, c1[:w], 0.0)
    l0, l1, c0, c1 = (jnp.where(skip, 0.0, value) for value in (l0, l1, c0, c1))

    a0 = product(l0, inv0)
    lower = factor[low:, :left]
    part = product_t(jnp.concatenate([a0, l1], axis=1), jnp.concatenate([lower, c1], axis=1))
    part_diag = raw_diag - product_t(a0, c0)
    sums = jnp.concatenate(
        [part[:w, :left], part[w:, :left], part_diag, part[:w, left:], part[w:, left:], raw_next, raw_r31],
        axis=1,
    )
    total_cols = sums.shape[1]
    swapped = lax.all_to_all(sums.reshape(rows, piece, total_cols), ROW, 0, 0)
    mine = jnp.sum(swapped, axis=0)
    total = lax.all_to_all(jnp.broadcast_to(mine[None], swapped.shape), ROW, 0, 0)
    total = total.reshape(w, total_cols)
    s0, y1 = total[:, :left], total[:, left : 2 * left]
    dsum, t01, x11, next31, r31 = (
        total[:, 2 * left + i * w : 2 * left + (i + 1) * w] for i in range(5)
    )

    d0, d1 = lower_inverse(inv0), lower_inverse(inv1)
    g0 = adjoint_diag(inv0, d0, dsum)
    a132 = product(next31 - t01 - product(g0, r31), inv1)
    t11 = product_t(inv1, x11 - product_t(r31, t01)) + product_t(a132, r31)
    g1 = adjoint_diag(inv1, d1, diag31 - t11)
    a1 = product(l1, inv1) - product(a0, product(r31, inv1))
    u1 = product_t(inv1, y1 - product_t(r31, s0))

    first_cols = jnp.where(skip, jnp.concatenate([g0, a0[w:]]), a0)
    second_cols = jnp.where(skip, jnp.concatenate([a132, a1[w:]]), a1)
    trail = adjoint[low:, :left] - product(
        jnp.concatenate([first_cols, second_cols], axis=1), factor_rows
    )
    top = trail[:w] - jnp.where(at_first, s0, 0.0)
    row31 = adjoint[w:low, :left] - u1 - product(
        jnp.concatenate([a132.T, g1], axis=1), factor_rows
    )
    row31 = jnp.where(p == last_p, row31, adjoint[w:low, :left])
    diag_skip = skip[:w]
    col0 = jnp.concatenate([jnp.where(at_first, halved_lower(g0), a0[:w]), a0[w:]])
    upd = jnp.concatenate([row31, top, trail[w:]], axis=0)
    new31 = jnp.concatenate(
        [jnp.where(p == last_p, halved_lower(g1), adjoint[w:low, left - w : left]), second_cols]
    )
    upd_last = jnp.where(q == last_q, new31, upd[:, left - w :])
    out = adjoint.at[w:, : left - w].set(upd[:, : left - w])
    out = out.at[w:, left - w : left].set(upd_last)
    out = out.at[low:, left : left + w].set(
        jnp.where(first, col0, adjoint[low:, left : left + w])
    )
    return out


def solution(mesh):
    grid = Mesh(mesh.devices.reshape(4, 4, 4, 2), ("z", "x", "y", "core"))
    return jax.shard_map(
        per_device,
        mesh=grid,
        in_specs=(P(ROW, COL), P(ROW, COL), P()),
        out_specs=P(ROW, COL),
        check_vma=False,
    )
```

```python
import functools

import jax
import jax.numpy as jnp
from jax import lax
from jax.experimental import pallas as pl
from jax.experimental.pallas import tpu as pltpu
from jax.sharding import PartitionSpec as P

ROW = "row"
COL = "col"
RING = 4
VMEM = pl.BlockSpec(memory_space=pltpu.VMEM)
HBM = pl.BlockSpec(memory_space=pltpu.HBM)


def product(left, right):
    return jnp.dot(left, right, precision=lax.Precision.HIGHEST, preferred_element_type=jnp.float32)


def split(value):
    high = value.astype(jnp.bfloat16)
    return high, (value - high.astype(jnp.float32)).astype(jnp.bfloat16)


def product_split(left, right_high, right_low):
    left_high, left_low = split(left)
    dot = functools.partial(jnp.dot, preferred_element_type=jnp.float32)
    return dot(left_high, right_high) + (dot(left_low, right_high) + dot(left_high, right_low))


def masks(width):
    rows = lax.broadcasted_iota(jnp.int32, (width, width), 0)
    cols = lax.broadcasted_iota(jnp.int32, (width, width), 1)
    return rows > cols, rows == cols


def tril(matrix):
    below, diag = masks(matrix.shape[0])
    return jnp.where(below | diag, matrix, 0.0)


def halved_lower(matrix):
    below, diag = masks(matrix.shape[0])
    return jnp.where(below, matrix, jnp.where(diag, 0.5 * matrix, 0.0))


def params(megabytes):
    return pltpu.CompilerParams(vmem_limit_bytes=megabytes << 20)


def cost(flops, bytes_accessed):
    return pl.CostEstimate(flops=flops, bytes_accessed=bytes_accessed, transcendentals=0)


def in_hbm(value):
    return pltpu.with_memory_space_constraint(value, pltpu.HBM)


def tile_shape(*shape):
    return jax.ShapeDtypeStruct(shape, jnp.float32)


def invert_kernel(tiles, out, out_t, power, total):
    width = tiles.shape[-1]
    below, diag = masks(width)
    scales = []
    for j in range(2):
        tile = tiles[j]
        out_t[j] = tile.T
        only = jnp.where(diag, tile, 0.0)
        power[j] = jnp.where(below, tile / jnp.sum(only, axis=1, keepdims=True), 0.0)
        total[j] = jnp.where(diag, 1.0, 0.0) - power[j]
        scales.append(1.0 / jnp.sum(only, axis=0, keepdims=True))

    @pl.loop(0, (width - 1).bit_length() - 1)
    def _(step):
        for j in range(2):
            power[j] = product(power[j], power[j])
        for j in range(2):
            total[j] = total[j] + product(total[j], power[j])

    for j in range(2):
        out[j] = (total[j] * scales[j]).T


def invert(tiles):
    w = tiles.shape[-1]
    return pl.pallas_call(
        invert_kernel,
        out_shape=(pltpu.HBM((2, w, w), jnp.float32),) * 2,
        in_specs=[VMEM],
        out_specs=(VMEM,) * 2,
        scratch_shapes=[pltpu.VMEM((2, w, w), jnp.float32)] * 2,
        compiler_params=params(10),
        cost_estimate=cost(28 * 12 * w**3, 1 << 20),
        name="invert",
    )(tiles)


def sums_kernel(even, odd, inv0, factor, out, a0_out, l1_out, high, low, small):
    step = pl.program_id(0)
    w = inv0.shape[0]
    rows = lax.axis_size(ROW)
    first = lax.axis_index(ROW) == 0
    per_step = w // (w * 4 // rows)
    cols = 4 * w // rows
    piece = w // rows

    @pl.when(step == 0)
    def _():
        l0, c0 = even[: 2 * w], even[2 * w : 4 * w]
        l1, c1 = odd[: 2 * w], odd[2 * w : 4 * w]
        skip = first & (lax.broadcasted_iota(jnp.int32, l0.shape, 0) < w)
        a0 = jnp.where(skip, 0.0, product(l0, inv0[...]))
        below = jnp.where(skip, 0.0, l1)
        a0_out[...] = a0
        l1_out[...] = below
        high[:, :w], low[:, :w] = split(a0)
        high[:, w:], low[:, w:] = split(below)
        a0_t, below_t = a0.T, below.T
        diag_high, diag_low = split(jnp.where(skip, 0.0, c0))
        next_high, next_low = split(jnp.where(skip, 0.0, c1))
        raw = jnp.where(first, l0[:w], 0.0)
        raw_next = jnp.where(first, l1[:w], 0.0)
        small[0] = raw - product_split(a0_t, diag_high, diag_low)
        small[1] = raw_next - product_split(a0_t, next_high, next_low)
        small[2] = product_split(below_t, next_high, next_low) - product(c1[:w].T, raw_next)

    part = product_split(factor[...].T, high[...], low[...])
    out[:, :cols, :] = part[:, :w].reshape(per_step, cols, w)
    out[:, cols : 2 * cols, :] = part[:, w:].reshape(per_step, cols, w)
    start = pl.multiple_of(step * (per_step * piece), per_step * piece)
    for j in range(3):
        lines = small[j, pl.ds(start, per_step * piece), :]
        at = 2 * cols + j * piece
        out[:, at : at + piece, :] = lines.reshape(per_step, piece, w)


def sums(even, odd, inv0, factor):
    w = inv0.shape[0]
    rows = lax.axis_size(ROW)
    height = 2 * (4 * w // rows) + 3 * (w // rows)
    const = lambda i: (0, 0)
    whole = lambda value: pl.BlockSpec(value.shape, const, pipeline_mode=pl.Buffered(1))
    return pl.pallas_call(
        sums_kernel,
        grid=(4,),
        out_shape=(pltpu.HBM((rows, height, w), jnp.float32),)
        + (pltpu.HBM((2 * w, w), jnp.float32),) * 2,
        in_specs=[whole(even), whole(odd), whole(inv0)]
        + [pl.BlockSpec((2 * w, w), lambda i: (1, i))],
        out_specs=(
            pl.BlockSpec((rows // 4, height, w), lambda i: (i, 0, 0)),
            pl.BlockSpec((2 * w, w), const),
            pl.BlockSpec((2 * w, w), const),
        ),
        scratch_shapes=[
            pltpu.VMEM((2 * w, 2 * w), jnp.bfloat16),
            pltpu.VMEM((2 * w, 2 * w), jnp.bfloat16),
            pltpu.VMEM((3, w, w), jnp.float32),
        ],
        compiler_params=params(14),
        cost_estimate=cost(4 << 30, 8 << 20),
        name="sums",
    )(even, odd, inv0, in_hbm(factor))


def middle_kernel(terms, r31, inv1, out, r31_v, inv1_v, out_v, sems):
    rows = terms.shape[0]
    cols = (terms.shape[1] - 3 * (inv1.shape[0] // rows)) // 2
    fetches = [
        pltpu.make_async_copy(r31, r31_v, sems.at[0]),
        pltpu.make_async_copy(inv1, inv1_v, sems.at[1]),
    ]
    for fetch in fetches:
        fetch.start()
    total = terms[0]
    for i in range(1, rows):
        total = total + terms[i]
    top = total[:cols]
    for fetch in fetches:
        fetch.wait()
    bottom = product(total[cols : 2 * cols] - product(top, r31_v[...]), inv1_v[...])
    out_v[0, :cols, :] = top
    out_v[1, :cols, :] = bottom
    for i in range(2):
        out_v[i, cols:, :] = total[2 * cols :]
    stores = [
        pltpu.make_async_copy(out_v.at[min(i, 1)], out.at[i], sems.at[2 + i]) for i in range(rows)
    ]
    for store in stores:
        store.start()
    for store in stores:
        store.wait()


def middle(terms, r31, inv1):
    rows, height, w = terms.shape
    cols = (height - 3 * (w // rows)) // 2
    return pl.pallas_call(
        middle_kernel,
        out_shape=pltpu.HBM((rows, height - cols, w), jnp.float32),
        in_specs=[VMEM, HBM, HBM],
        out_specs=HBM,
        scratch_shapes=[
            pltpu.VMEM((w, w), jnp.float32),
            pltpu.VMEM((w, w), jnp.float32),
            pltpu.VMEM((2, height - cols, w), jnp.float32),
            pltpu.SemaphoreType.DMA((2 + rows,)),
        ],
        compiler_params=params(10),
        cost_estimate=cost(1 << 28, 6 << 20),
        name="middle",
    )(terms, in_hbm(r31), in_hbm(inv1))


def trail_kernel(adj, a0, l1, inv1, r31, own, down, up, across_first, across_second, out, r_high, r_low, r31_inv):
    step = pl.program_id(0)
    w = inv1.shape[0]
    left = 4 * w
    q = lax.axis_index(COL)
    last_q = lax.axis_size(COL) - 1
    z = lax.axis_index(ROW) // RING
    out[...] = adj[...]

    @pl.when(step == 0)
    def _():
        r31_inv[...] = product(r31[...], inv1[...])
        quarter = w // RING
        for j in range(2):
            values = (own[j], down[j], (across_first, across_second)[j][...], up[j])
            for k, value in enumerate(values):
                start = pl.multiple_of(j * w + lax.rem(z + k, RING) * quarter, quarter)
                high, low = split(value)
                r_high[pl.ds(start, quarter), :] = high
                r_low[pl.ds(start, quarter), :] = low

    @pl.when(step >= pl.num_programs(0) // 2)
    def _():
        first = a0[...]
        second = product(l1[...], inv1[...]) - product(first, r31_inv[...])
        lhs = jnp.concatenate([first, second], axis=1)
        out[:, :left] = adj[:, :left] - product_split(lhs, r_high[...], r_low[...])

        @pl.when(q == 0)
        def _():
            out[:, left : left + w] = first

        @pl.when(q == last_q)
        def _():
            out[:, left - w : left] = second


def trail(adjoint, a0, l1, inv1, r31, *pieces):
    rows, cols = adjoint.shape
    w = inv1.shape[0]
    steps = 8
    blk = rows // steps
    low = lambda i: (jnp.maximum(i - steps // 2, 0), 0)
    const = lambda i: (0, 0)
    one = pl.Buffered(1)
    panel = pltpu.HBM((2 * w, 4 * w), jnp.bfloat16)
    return pl.pallas_call(
        trail_kernel,
        grid=(steps,),
        out_shape=(tile_shape(*adjoint.shape), panel, panel),
        in_specs=[
            pl.BlockSpec((blk, cols), lambda i: (i, 0)),
            pl.BlockSpec((blk, w), low),
            pl.BlockSpec((blk, w), low),
            pl.BlockSpec(inv1.shape, const, pipeline_mode=one),
            pl.BlockSpec(r31.shape, const, pipeline_mode=one),
        ]
        + [VMEM] * len(pieces),
        out_specs=(
            pl.BlockSpec((blk, cols), lambda i: (i, 0)),
            pl.BlockSpec(panel.shape, const),
            pl.BlockSpec(panel.shape, const),
        ),
        scratch_shapes=[pltpu.VMEM((w, w), jnp.float32)],
        compiler_params=params(16),
        cost_estimate=cost(4 << 30, 22 << 20),
        name="trail",
    )(in_hbm(adjoint), a0, l1, inv1, r31, *pieces)


def final_kernel(
    base, got, inverse, inverse_t, diag_t, diag31, r31, r_high, r_low, out,
    got_v, inverse_v, inverse_tv, diag_tv, diag31_v, r31_v, r_high_v, r_low_v, rows_buf, tile_buf, sems
):
    w = inverse.shape[-1]
    left = 4 * w
    p = lax.axis_index(ROW)
    q = lax.axis_index(COL)
    rows = got.shape[0]
    last_p = rows - 1
    last_q = lax.axis_size(COL) - 1
    piece = w // rows
    cols = got.shape[1] - 3 * piece
    at_root = (p == 0) | (p == last_p)

    @pl.when(at_root)
    def _():
        start = jnp.where(p == 0, 2 * w, w)
        tiles = pl.ds(cols, 3 * piece)
        moves = [
            (got.at[:, tiles, :], got_v.at[:, tiles, :]),
            (diag_t, diag_tv),
            (inverse_t, inverse_tv),
            (inverse, inverse_v),
            (r31, r31_v),
            (diag31, diag31_v),
            (r_high, r_high_v),
            (r_low, r_low_v),
            (base.at[pl.ds(start, w), pl.ds(0, left)], rows_buf),
            (got.at[:, pl.ds(0, cols), :], got_v.at[:, pl.ds(0, cols), :]),
        ]
        fetches = [pltpu.make_async_copy(src, dst, sems.at[i]) for i, (src, dst) in enumerate(moves)]
        for fetch in fetches:
            fetch.start()
        for fetch in fetches[:6]:
            fetch.wait()
        dsum, t01, x11 = (
            got_v[:, cols + j * piece : cols + (j + 1) * piece, :].reshape(w, w) for j in range(3)
        )

        def adjoint_diag(j, dprime):
            inner = halved_lower(product(diag_tv[j], tril(dprime)))
            wmat = product(product(inverse_tv[j], inner), inverse_v[j])
            return wmat + wmat.T

        corner = r31_v[...]
        side = product(inverse_tv[1], x11 + product(corner.T, t01))
        g0 = adjoint_diag(0, dsum)
        a132 = product(t01 - product(g0, corner), inverse_v[1])
        t11 = side + product(a132.T, corner)
        g1 = adjoint_diag(1, diag31_v[...] - t11)
        lhs = jnp.where(
            p == 0,
            jnp.concatenate([g0, a132], axis=1),
            jnp.concatenate([a132.T, g1], axis=1),
        )
        for fetch in fetches[6:]:
            fetch.wait()
        update = product_split(lhs, r_high_v[...], r_low_v[...])
        rows_buf[...] = rows_buf[...] - update - got_v[:, :cols, :].reshape(left, w).T

        @pl.when(q == last_q)
        def _():
            rows_buf[:, left - w :] = jnp.where(p == 0, a132, halved_lower(g1))

        store = pltpu.make_async_copy(
            rows_buf, out.at[pl.ds(start, w), pl.ds(0, left)], sems.at[len(moves)]
        )
        store.start()

        @pl.when((p == 0) & (q == 0))
        def _():
            tile_buf[...] = halved_lower(g0)
            corner_store = pltpu.make_async_copy(
                tile_buf, out.at[pl.ds(2 * w, w), pl.ds(left, w)], sems.at[len(moves) + 1]
            )
            corner_store.start()
            corner_store.wait()

        store.wait()


def final(base, *operands):
    w = operands[1].shape[-1]
    return pl.pallas_call(
        final_kernel,
        out_shape=tile_shape(*base.shape),
        in_specs=[HBM] * (1 + len(operands)),
        out_specs=HBM,
        scratch_shapes=[pltpu.VMEM(value.shape, value.dtype) for value in operands]
        + [
            pltpu.VMEM((w, 4 * w), jnp.float32),
            pltpu.VMEM((w, w), jnp.float32),
            pltpu.SemaphoreType.DMA((12,)),
        ],
        input_output_aliases={0: 0},
        compiler_params=params(16),
        cost_estimate=cost(6 << 30, 8 << 20),
        name="final",
    )(base, *[in_hbm(value) for value in operands])


def column_near(block):
    last = lax.axis_size(COL) - 1
    near = lax.ppermute(block, COL, [(0, 2), (last, last - 2)])
    far = lax.ppermute(block, COL, [(0, last - 1), (last, 1)])
    return near, far


def column_across(block, near, far):
    q = lax.axis_index(COL)
    last = lax.axis_size(COL) - 1
    half = block.shape[0] // 2
    upper = lax.ppermute(near[:half], COL, [(2, 4), (last - 2, last - 4)])
    lower = lax.ppermute(far[half:], COL, [(last - 1, 4), (1, last - 4)])
    return jnp.where(
        (q == 0) | (q == last),
        block,
        jnp.where(
            (q == 2) | (q == last - 2),
            near,
            jnp.where((q == 1) | (q == last - 1), far, jnp.concatenate([upper, lower], axis=0)),
        ),
    )


def column_swap(mine):
    theirs = lax.ppermute(mine, COL, [(i, i ^ 1) for i in range(lax.axis_size(COL))])
    even = lax.axis_index(COL) % 2 == 0
    return jnp.where(even, mine, theirs), jnp.where(even, theirs, mine)


def row_quarters(block):
    p = lax.axis_index(ROW)
    last = lax.axis_size(ROW) - 1
    top = RING - 1
    quarters = block.reshape(RING, -1, block.shape[1])
    first = p == 0
    near = lax.ppermute(
        jnp.where(first, quarters[1], quarters[top - 1]), ROW, [(0, RING), (last, last - RING)]
    )
    far = lax.ppermute(jnp.where(first, quarters[top], quarters[0]), ROW, [(0, last - top), (last, top)])
    across = lax.ppermute(
        jnp.where(first, quarters[2], quarters[1]), ROW, [(0, 2 * RING), (last, last - 2 * RING)]
    )
    mine = jnp.where(first, quarters[0], quarters[top])
    mine = jnp.where((p == RING) | (p == last - RING), near, mine)
    mine = jnp.where((p == last - top) | (p == top), far, mine)
    return jnp.where((p == 2 * RING) | (p == last - 2 * RING), across, mine)


def row_spread(mine):
    top = RING - 1
    x = lax.axis_index(ROW) % RING
    lines = range(0, lax.axis_size(ROW), RING)
    near = lax.ppermute(mine, ROW, [e for s in lines for e in ((s, s + 1), (s + top, s + top - 1))])
    far = lax.ppermute(mine, ROW, [e for s in lines for e in ((s, s + top), (s + top, s))])
    across = lax.ppermute(mine, ROW, [e for s in lines for e in ((s, s + 2), (s + top, s + top - 2))])
    from_first = jnp.where(x == 0, mine, jnp.where(x == 1, near, jnp.where(x == 2, across, far)))
    from_last = jnp.where(x == top, mine, jnp.where(x == 2, near, jnp.where(x == 1, across, far)))
    return jnp.stack([from_first, from_last])


def ring_pairs(step):
    count = lax.axis_size(ROW)
    return [(i, (i + step * RING) % count) for i in range(count)]


def per_device(factor, adjoint, inverse):
    w = inverse.shape[-1]
    rows = lax.axis_size(ROW)
    p = lax.axis_index(ROW)
    q = lax.axis_index(COL)
    low, left = 2 * w, 4 * w

    start = jnp.where(q == 0, left, left - w)
    adj_col = lax.dynamic_slice(adjoint, (low, start), (low, w))
    fac_col = lax.dynamic_slice(factor, (low, start), (low, w))
    block = jnp.concatenate([adj_col, fac_col, adjoint[w:low, left - w : left]], axis=0)
    row_block = lax.dynamic_slice(factor, (jnp.where(p == 0, low, w), 0), (w, left))
    quarter = row_quarters(row_block)
    block, quarter = lax.optimization_barrier((block, quarter))
    near, far = column_near(block)
    own = row_spread(quarter)
    near, far, own = lax.optimization_barrier((near, far, own))
    mine = column_across(block, near, far)
    up = lax.ppermute(own, ROW, ring_pairs(1))
    down = lax.ppermute(own, ROW, ring_pairs(-1))
    even, odd = column_swap(mine)
    terms, a0, l1_below = sums(even, odd, inverse[0], factor)
    up, down, l1_below = lax.optimization_barrier((up, down, l1_below))
    across_first = lax.ppermute(up[0], ROW, ring_pairs(1))
    across_second = lax.ppermute(down[1], ROW, ring_pairs(-1))
    terms, across_first, across_second = lax.optimization_barrier((terms, across_first, across_second))
    terms = lax.all_to_all(terms, ROW, 0, 0)
    diag_t, inverse_t = invert(inverse)

    z = p // RING
    corner = [value[..., left - w :].reshape(-1, w) for value in (own[0], down[0], across_first, up[0])]
    corner = jnp.concatenate(corner, axis=0)
    corner = column_swap(column_across(corner, *column_near(corner)))[1]
    r31 = lax.dynamic_slice(
        jnp.concatenate([corner, corner], axis=0), ((RING - z) % RING * (w // RING), 0), (w, w)
    )
    base, r_high, r_low = trail(
        adjoint, a0, l1_below, inverse[1], r31, own, down, up, across_first, across_second
    )
    terms, diag_t, inverse_t = lax.optimization_barrier((terms, diag_t, inverse_t))
    shares = lax.all_to_all(middle(terms, r31, inverse[1]), ROW, 0, 0)
    return final(base, shares, inverse, inverse_t, diag_t, odd[2 * low :], r31, r_high, r_low)


def solution(mesh):
    return jax.shard_map(
        per_device,
        mesh=mesh,
        in_specs=(P(ROW, COL), P(ROW, COL), P()),
        out_specs=P(ROW, COL),
        check_vma=False,
    )
```

```python
import functools

import jax
import jax.numpy as jnp
from jax import lax
from jax.experimental import pallas as pl
from jax.experimental.pallas import tpu as pltpu
from jax.sharding import PartitionSpec as P

ROW = "row"
COL = "col"
RING = 4
VMEM = pl.BlockSpec(memory_space=pltpu.VMEM)
HBM = pl.BlockSpec(memory_space=pltpu.HBM)


def product(left, right):
    return jnp.dot(left, right, precision=lax.Precision.HIGHEST, preferred_element_type=jnp.float32)


def split(value):
    high = value.astype(jnp.bfloat16)
    return high, (value - high.astype(jnp.float32)).astype(jnp.bfloat16)


def product_split(left, right_high, right_low):
    left_high, left_low = split(left)
    dot = functools.partial(jnp.dot, preferred_element_type=jnp.float32)
    return dot(left_high, right_high) + (dot(left_low, right_high) + dot(left_high, right_low))


def masks(width):
    rows = lax.broadcasted_iota(jnp.int32, (width, width), 0)
    cols = lax.broadcasted_iota(jnp.int32, (width, width), 1)
    return rows > cols, rows == cols


def tril(matrix):
    below, diag = masks(matrix.shape[0])
    return jnp.where(below | diag, matrix, 0.0)


def halved_lower(matrix):
    below, diag = masks(matrix.shape[0])
    return jnp.where(below, matrix, jnp.where(diag, 0.5 * matrix, 0.0))


def params(megabytes):
    return pltpu.CompilerParams(vmem_limit_bytes=megabytes << 20)


def cost(flops, bytes_accessed):
    return pl.CostEstimate(flops=flops, bytes_accessed=bytes_accessed, transcendentals=0)


def in_hbm(value):
    return pltpu.with_memory_space_constraint(value, pltpu.HBM)


def tile_shape(*shape):
    return jax.ShapeDtypeStruct(shape, jnp.float32)


def invert_kernel(tiles, adj, a0, out, out_t, base, power, total, held, sems):
    width = tiles.shape[-1]
    low, left = 2 * width, 4 * width
    q = lax.axis_index(COL)
    half = low // 2
    keep = [(slice(i * half, (i + 1) * half), slice(0, adj.shape[1])) for i in range(2)]
    keep += [(slice(low + i * half, low + (i + 1) * half), slice(left, adj.shape[1])) for i in range(2)]
    stage = [held.at[i, :, slice(0, at[1].stop - at[1].start)] for i, at in enumerate(keep)]
    loads = [pltpu.make_async_copy(adj.at[at], dst, sems.at[i]) for i, (at, dst) in enumerate(zip(keep, stage))]
    stores = [pltpu.make_async_copy(src, base.at[at], sems.at[i + 4]) for i, (at, src) in enumerate(zip(keep, stage))]
    for load in loads:
        load.start()
    below, diag = masks(width)
    scales = []
    for j in range(2):
        tile = tiles[j]
        out_t[j] = tile.T
        only = jnp.where(diag, tile, 0.0)
        power[j] = jnp.where(below, tile / jnp.sum(only, axis=1, keepdims=True), 0.0)
        total[j] = jnp.where(diag, 1.0, 0.0) - power[j]
        scales.append(1.0 / jnp.sum(only, axis=0, keepdims=True))

    for load in loads:
        load.wait()

    @pl.when(q == 0)
    def _():
        for i in range(2):
            held[2 + i, :, :width] = a0[i * half : (i + 1) * half, :]

    for store in stores:
        store.start()

    @pl.loop(0, (width - 1).bit_length() - 1)
    def _(step):
        for j in range(2):
            power[j] = product(power[j], power[j])
        for j in range(2):
            total[j] = total[j] + product(total[j], power[j])

    for j in range(2):
        out[j] = (total[j] * scales[j]).T
    for store in stores:
        store.wait()


def invert(tiles, adjoint, a0):
    w = tiles.shape[-1]
    return pl.pallas_call(
        invert_kernel,
        out_shape=(pltpu.HBM((2, w, w), jnp.float32),) * 2 + (pltpu.HBM(adjoint.shape, jnp.float32),),
        in_specs=[VMEM, HBM, VMEM],
        out_specs=(VMEM,) * 2 + (HBM,),
        scratch_shapes=[pltpu.VMEM((2, w, w), jnp.float32)] * 2
        + [pltpu.VMEM((4, w, adjoint.shape[1]), jnp.float32), pltpu.SemaphoreType.DMA((8,))],
        compiler_params=params(14),
        cost_estimate=cost(28 * 12 * w**3, 1 << 20),
        name="invert",
    )(tiles, in_hbm(adjoint), in_hbm(a0))


def corner_kernel(own, down, up, across_first, out, held, sems):
    w = out.shape[0]
    quarter = w // RING
    z = lax.axis_index(ROW) // RING
    left = own.shape[-1]
    tile = (slice(None), slice(left - w, left))
    sources = (own.at[(0,) + tile], down.at[(0,) + tile], across_first.at[tile], up.at[(0,) + tile])
    fetches = [pltpu.make_async_copy(src, held.at[k], sems.at[k]) for k, src in enumerate(sources)]
    for fetch in fetches:
        fetch.start()
    for fetch in fetches:
        fetch.wait()
    for k in range(RING):
        start = pl.multiple_of(lax.rem(z + k, RING) * quarter, quarter)
        out[pl.ds(start, quarter), :] = held[k]


def gather_corner(own, down, up, across_first):
    w = own.shape[1] * RING
    return pl.pallas_call(
        corner_kernel,
        out_shape=tile_shape(w, w),
        in_specs=[HBM] * 4,
        out_specs=VMEM,
        scratch_shapes=[
            pltpu.VMEM((RING, w // RING, w), jnp.float32),
            pltpu.SemaphoreType.DMA((RING,)),
        ],
        compiler_params=params(4),
        cost_estimate=cost(1 << 10, 1 << 19),
        name="corner",
    )(*[in_hbm(value) for value in (own, down, up, across_first)])


def small_rows(w, rows):
    return -(-3 * (w // lax.axis_size(COL) // rows) // 8) * 8


def sums_kernel(even_top, even_bottom, odd_top, odd_bottom, inv0, factor, out, a0_out, l1_out, high, low, small, tall):
    step = pl.program_id(0)
    w = inv0.shape[0]
    rows = lax.axis_size(ROW)
    first = lax.axis_index(ROW) == 0
    per_step = w // (w * 4 // rows)
    cols = 4 * w // rows
    piece = small.shape[1] // rows

    @pl.when(step == 0)
    def _():
        cut = w // 2
        l0, l1 = even_top[: 2 * w], odd_top[: 2 * w]
        c0 = jnp.concatenate([even_top[2 * w :], even_bottom[: 2 * w - cut]], axis=0)
        c1 = jnp.concatenate([odd_top[2 * w :], odd_bottom[: 2 * w - cut]], axis=0)
        skip = first & (lax.broadcasted_iota(jnp.int32, l0.shape, 0) < w)
        a0 = jnp.where(skip, 0.0, product(l0, inv0[...]))
        below = jnp.where(skip, 0.0, l1)
        a0_out[...] = a0
        l1_out[...] = below
        high[:, :w], low[:, :w] = split(a0)
        high[:, w:], low[:, w:] = split(below)
        tall[0] = a0.T
        tall[1] = below.T
        share = w // lax.axis_size(COL)
        mine = pl.ds(pl.multiple_of(lax.axis_index(COL) * share, share), share)
        diag_below = jnp.where(skip, 0.0, c0)
        next_below = jnp.where(skip, 0.0, c1)
        raw_next = jnp.where(first, l1[:w], 0.0)
        tall[2, :, :w] = c1[:w].T
        small[0] = jnp.where(first, even_top[mine, :], 0.0) - product(tall[0, mine, :], diag_below)
        small[1] = jnp.where(first, odd_top[mine, :], 0.0) - product(tall[0, mine, :], next_below)
        small[2] = product(tall[1, mine, :], next_below) - product(tall[2, mine, :w], raw_next)

    part = product_split(factor[...].T, high[...], low[...])
    out[:, :cols, :] = part[:, :w].reshape(per_step, cols, w)
    out[:, cols : 2 * cols, :] = part[:, w:].reshape(per_step, cols, w)
    lines = per_step * piece
    for j in range(3):
        part = small[j, pl.ds(pl.multiple_of(step * lines, lines), lines), :]
        at = 2 * cols + j * piece
        out[:, at : at + piece, :] = part.reshape(per_step, piece, w)
    at = 2 * cols + 3 * piece
    out[:, at:, :] = jnp.zeros((per_step, out.shape[1] - at, w), jnp.float32)


def sums(even_top, even_bottom, odd_top, odd_bottom, inv0, factor):
    w = inv0.shape[0]
    rows = lax.axis_size(ROW)
    share = w // lax.axis_size(COL)
    height = 2 * (4 * w // rows) + small_rows(w, rows)
    const = lambda i: (0, 0)
    whole = lambda value: pl.BlockSpec(value.shape, const, pipeline_mode=pl.Buffered(1))
    return pl.pallas_call(
        sums_kernel,
        grid=(4,),
        out_shape=(pltpu.HBM((rows, height, w), jnp.float32),)
        + (pltpu.HBM((2 * w, w), jnp.float32),) * 2,
        in_specs=[whole(even_top), whole(even_bottom), whole(odd_top), whole(odd_bottom), whole(inv0)]
        + [pl.BlockSpec((2 * w, w), lambda i: (1, i))],
        out_specs=(
            pl.BlockSpec((rows // 4, height, w), lambda i: (i, 0, 0)),
            pl.BlockSpec((2 * w, w), const),
            pl.BlockSpec((2 * w, w), const),
        ),
        scratch_shapes=[
            pltpu.VMEM((2 * w, 2 * w), jnp.bfloat16),
            pltpu.VMEM((2 * w, 2 * w), jnp.bfloat16),
            pltpu.VMEM((3, share, w), jnp.float32),
            pltpu.VMEM((3, w, 2 * w), jnp.float32),
        ],
        compiler_params=params(14),
        cost_estimate=cost(4 << 30, 8 << 20),
        name="sums",
    )(even_top, even_bottom, odd_top, odd_bottom, inv0, in_hbm(factor))


def middle_kernel(terms, r31, inv1, out, out_small, r31_v, inv1_v, out_v, small_v, sems):
    rows, cols = out.shape[:2]
    fetches = [
        pltpu.make_async_copy(r31, r31_v, sems.at[0]),
        pltpu.make_async_copy(inv1, inv1_v, sems.at[1]),
    ]
    for fetch in fetches:
        fetch.start()
    small = terms[0, 2 * cols :, :]
    for i in range(1, rows):
        small = small + terms[i, 2 * cols :, :]
    for i in range(rows):
        small_v[i] = small
    stores = [pltpu.make_async_copy(small_v, out_small, sems.at[2])]
    stores[0].start()
    total = terms[0, : 2 * cols, :]
    for i in range(1, rows):
        total = total + terms[i, : 2 * cols, :]
    top = total[:cols]
    for fetch in fetches:
        fetch.wait()
    out_v[0] = top
    out_v[1] = product(total[cols:] - product(top, r31_v[...]), inv1_v[...])
    stores += [pltpu.make_async_copy(out_v.at[min(i, 1)], out.at[i], sems.at[3 + i]) for i in range(rows)]
    for store in stores[1:]:
        store.start()
    for store in stores:
        store.wait()


def middle(terms, r31, inv1):
    rows, height, w = terms.shape
    small = small_rows(w, rows)
    cols = (height - small) // 2
    return pl.pallas_call(
        middle_kernel,
        out_shape=(pltpu.HBM((rows, cols, w), jnp.float32), pltpu.HBM((rows, small, w), jnp.float32)),
        in_specs=[VMEM, HBM, HBM],
        out_specs=(HBM, HBM),
        scratch_shapes=[
            pltpu.VMEM((w, w), jnp.float32),
            pltpu.VMEM((w, w), jnp.float32),
            pltpu.VMEM((2, cols, w), jnp.float32),
            pltpu.VMEM((rows, small, w), jnp.float32),
            pltpu.SemaphoreType.DMA((3 + rows,)),
        ],
        compiler_params=params(10),
        cost_estimate=cost(1 << 28, 6 << 20),
        name="middle",
    )(terms, in_hbm(r31), in_hbm(inv1))


def trail_kernel(
    adj, a0, l1, inv1, r31, own, down, up, across_first, across_second, base, out, r_high, r_low,
    small, own_v, down_v, up_v, first_v, second_v, sems
):
    step = pl.program_id(0)
    w = inv1.shape[0]
    left = 4 * w
    q = lax.axis_index(COL)
    last_q = lax.axis_size(COL) - 1
    z = lax.axis_index(ROW) // RING

    @pl.when(step == 0)
    def _():
        sources = (own, down, up, across_first, across_second)
        targets = (own_v, down_v, up_v, first_v, second_v)
        fetches = [
            pltpu.make_async_copy(src, dst, sems.at[i]) for i, (src, dst) in enumerate(zip(sources, targets))
        ]
        for fetch in fetches:
            fetch.start()
        small[0], small[1] = split(inv1[...])
        small[2], small[3] = split(product(r31[...], inv1[...]))
        for fetch in fetches:
            fetch.wait()
        quarter = w // RING
        for j in range(2):
            values = (own_v[j], down_v[j], (first_v, second_v)[j][...], up_v[j])
            for k, value in enumerate(values):
                start = pl.multiple_of(j * w + lax.rem(z + k, RING) * quarter, quarter)
                high, low = split(value)
                r_high[pl.ds(start, quarter), :] = high
                r_low[pl.ds(start, quarter), :] = low

    first = a0[...]
    second = product_split(l1[...], small[0], small[1]) - product_split(first, small[2], small[3])
    lhs = jnp.concatenate([first, second], axis=1)
    out[...] = adj[...] - product_split(lhs, r_high[...], r_low[...])

    @pl.when(q == last_q)
    def _():
        out[:, left - w :] = second


def trail(adjoint, base, a0, l1, inv1, r31, *pieces):
    rows, cols = adjoint.shape
    w = inv1.shape[0]
    steps = 4
    blk = rows // 2 // steps
    low = lambda i: (i, 0)
    block = lambda i: (steps + i, 0)
    const = lambda i: (0, 0)
    one = pl.Buffered(1)
    panel = pltpu.HBM((2 * w, 4 * w), jnp.bfloat16)
    return pl.pallas_call(
        trail_kernel,
        grid=(steps,),
        out_shape=(pltpu.HBM(adjoint.shape, jnp.float32), panel, panel),
        in_specs=[
            pl.BlockSpec((blk, 4 * w), block),
            pl.BlockSpec((blk, w), low),
            pl.BlockSpec((blk, w), low),
            pl.BlockSpec(inv1.shape, const, pipeline_mode=one),
            pl.BlockSpec(r31.shape, const, pipeline_mode=one),
        ]
        + [HBM] * (len(pieces) + 1),
        out_specs=(
            pl.BlockSpec((blk, 4 * w), block),
            pl.BlockSpec(panel.shape, const),
            pl.BlockSpec(panel.shape, const),
        ),
        scratch_shapes=[pltpu.VMEM((4, w, w), jnp.bfloat16)]
        + [pltpu.VMEM(piece.shape, jnp.float32) for piece in pieces]
        + [pltpu.SemaphoreType.DMA((len(pieces),))],
        input_output_aliases={5 + len(pieces): 0},
        compiler_params=params(16),
        cost_estimate=cost(4 << 30, 10 << 20),
        name="trail",
    )(
        in_hbm(adjoint),
        in_hbm(a0),
        in_hbm(l1),
        in_hbm(inv1),
        in_hbm(r31),
        *[in_hbm(piece) for piece in pieces],
        in_hbm(base),
    )


def chain_kernel(
    mine, before, after, across, theirs, inverse, inverse_t, diag_t, diag31, r31, lhs, corner, diag, tiles
):
    w = inverse.shape[-1]
    rows = mine.shape[0]
    p = lax.axis_index(ROW)
    q = lax.axis_index(COL)
    share = w // lax.axis_size(COL)
    piece = share // rows

    @pl.when((p == 0) | (p == rows - 1))
    def _():
        core = lax.rem(q, 2)
        for k, shared in ((0, mine), (1, after), (2, across), (3, before)):
            chip = lax.rem(q // 2 + k, RING)
            for other in range(2):
                at = chip * 2 + (1 - core if other else core)
                target = pl.ds(pl.multiple_of(at * share, share), share)
                for j in range(3):
                    lines = slice(j * piece, (j + 1) * piece)
                    value = theirs[k, :, lines, :] if other else shared[:, lines, :]
                    tiles[j, target, :] = value.reshape(share, w)
        t01, x11 = tiles[1], tiles[2]

        def adjoint_diag(j, dprime):
            inner = halved_lower(product(diag_t[j], tril(dprime)))
            wmat = product(product(inverse_t[j], inner), inverse[j])
            return wmat + wmat.T

        known = r31[...]
        side = product(inverse_t[1], x11 + product(known.T, t01))
        g0 = adjoint_diag(0, tiles[0])
        a132 = product(t01 - product(g0, known), inverse[1])
        diag[...] = halved_lower(g0)

        @pl.when(p == 0)
        def _():
            lhs[:, :w] = g0
            lhs[:, w:] = a132
            corner[...] = a132

        @pl.when(p != 0)
        def _():
            a132_t = a132.T
            g1 = adjoint_diag(1, diag31[...] - side - product(a132_t, known))
            lhs[:, :w] = a132_t
            lhs[:, w:] = g1
            corner[...] = halved_lower(g1)


def chain(*operands):
    w = operands[5].shape[-1]
    return pl.pallas_call(
        chain_kernel,
        out_shape=tuple(pltpu.HBM((w, n * w), jnp.float32) for n in (2, 1, 1)),
        in_specs=[VMEM] * len(operands),
        out_specs=(VMEM,) * 3,
        scratch_shapes=[pltpu.VMEM((3, w, w), jnp.float32)],
        compiler_params=params(14),
        cost_estimate=cost(1 << 20, 1 << 10),
        name="chain",
    )(*operands)


def final_kernel(base, got, lhs, corner, diag, r_high, r_low, out, *scratch):
    got_v, lhs_v, corner_v, diag_v, r_high_v, r_low_v, rows_buf, sems = scratch
    rows, cols, w = got.shape
    left = 4 * w
    p = lax.axis_index(ROW)
    q = lax.axis_index(COL)
    last_q = lax.axis_size(COL) - 1

    @pl.when((p == 0) | (p == rows - 1))
    def _():
        start = jnp.where(p == 0, 2 * w, w)
        region = (pl.ds(start, w), pl.ds(0, left))
        moves = [
            (lhs, lhs_v),
            (r_high, r_high_v),
            (r_low, r_low_v),
            (base.at[region], rows_buf),
            (got, got_v),
            (corner, corner_v),
            (diag, diag_v),
        ]
        fetches = [pltpu.make_async_copy(src, dst, sems.at[i]) for i, (src, dst) in enumerate(moves)]
        for fetch in fetches:
            fetch.start()
        for fetch in fetches:
            fetch.wait()
        stores = []
        for j in range(4):
            at = slice(j * w, (j + 1) * w)
            piece = rows // 4
            value = rows_buf[:, at] - got_v[j * piece : (j + 1) * piece].reshape(w, w).T
            rows_buf[:, at] = value - product_split(lhs_v[...], r_high_v[:, at], r_low_v[:, at])
            if j == 3:

                @pl.when(q == last_q)
                def _():
                    rows_buf[:, at] = corner_v[...]

            stores.append(
                pltpu.make_async_copy(
                    rows_buf.at[:, at], out.at[pl.ds(start, w), at], sems.at[len(moves) + j]
                )
            )
            stores[-1].start()

        @pl.when((p == 0) & (q == 0))
        def _():
            store = pltpu.make_async_copy(
                diag_v, out.at[pl.ds(2 * w, w), pl.ds(left, w)], sems.at[len(moves) + 4]
            )
            store.start()
            store.wait()

        for store in stores:
            store.wait()


def final(base, *operands):
    w = operands[1].shape[0]
    return pl.pallas_call(
        final_kernel,
        out_shape=tile_shape(*base.shape),
        in_specs=[HBM] * (1 + len(operands)),
        out_specs=HBM,
        scratch_shapes=[
            pltpu.VMEM(operands[i].shape, operands[i].dtype) for i in range(len(operands))
        ]
        + [pltpu.VMEM((w, 4 * w), jnp.float32), pltpu.SemaphoreType.DMA((12,))],
        input_output_aliases={0: 0},
        compiler_params=params(16),
        cost_estimate=cost(2 << 30, 8 << 20),
        name="final",
    )(base, *[in_hbm(value) for value in operands])


def column_hops(top, bottom):
    q = lax.axis_index(COL)
    last = lax.axis_size(COL) - 1
    near, far = [(0, 2), (last, last - 2)], [(0, last - 1), (last, 1)]
    near_top = lax.ppermute(top, COL, near)
    far_bottom = lax.ppermute(bottom, COL, far)
    near_bottom = lax.ppermute(bottom, COL, near)
    far_top = lax.ppermute(top, COL, far)
    upper = lax.ppermute(near_top, COL, [(2, 4), (last - 2, last - 4)])
    lower = lax.ppermute(far_bottom, COL, [(last - 1, 4), (1, last - 4)])

    def choose(own, near_value, far_value, across):
        value = jnp.where((q == 1) | (q == last - 1), far_value, across)
        value = jnp.where((q == 2) | (q == last - 2), near_value, value)
        return jnp.where((q == 0) | (q == last), own, value)

    return choose(top, near_top, far_top, upper), choose(bottom, near_bottom, far_bottom, lower)


def column_swap(mine):
    theirs = lax.ppermute(mine, COL, [(i, i ^ 1) for i in range(lax.axis_size(COL))])
    even = lax.axis_index(COL) % 2 == 0
    return jnp.where(even, mine, theirs), jnp.where(even, theirs, mine)


def row_quarters(block):
    p = lax.axis_index(ROW)
    last = lax.axis_size(ROW) - 1
    top = RING - 1
    quarters = block.reshape(RING, -1, block.shape[1])
    first = p == 0
    near = lax.ppermute(
        jnp.where(first, quarters[1], quarters[top - 1]), ROW, [(0, RING), (last, last - RING)]
    )
    far = lax.ppermute(jnp.where(first, quarters[top], quarters[0]), ROW, [(0, last - top), (last, top)])
    across = lax.ppermute(
        jnp.where(first, quarters[2], quarters[1]), ROW, [(0, 2 * RING), (last, last - 2 * RING)]
    )
    mine = jnp.where(first, quarters[0], quarters[top])
    mine = jnp.where((p == RING) | (p == last - RING), near, mine)
    mine = jnp.where((p == last - top) | (p == top), far, mine)
    return jnp.where((p == 2 * RING) | (p == last - 2 * RING), across, mine)


def row_spread(mine):
    top = RING - 1
    x = lax.axis_index(ROW) % RING
    lines = range(0, lax.axis_size(ROW), RING)
    near = lax.ppermute(mine, ROW, [e for s in lines for e in ((s, s + 1), (s + top, s + top - 1))])
    far = lax.ppermute(mine, ROW, [e for s in lines for e in ((s, s + top), (s + top, s))])
    across = lax.ppermute(mine, ROW, [e for s in lines for e in ((s, s + 2), (s + top, s + top - 2))])
    from_first = jnp.where(x == 0, mine, jnp.where(x == 1, near, jnp.where(x == 2, across, far)))
    from_last = jnp.where(x == top, mine, jnp.where(x == 2, near, jnp.where(x == 1, across, far)))
    return jnp.stack([from_first, from_last])


def ring_pairs(step):
    count = lax.axis_size(ROW)
    return [(i, (i + step * RING) % count) for i in range(count)]


def per_device(factor, adjoint, inverse):
    w = inverse.shape[-1]
    rows = lax.axis_size(ROW)
    p = lax.axis_index(ROW)
    q = lax.axis_index(COL)
    low, left = 2 * w, 4 * w

    start = jnp.where(q == 0, left, left - w)
    adj_col = lax.dynamic_slice(adjoint, (low, start), (low, w))
    fac_col = lax.dynamic_slice(factor, (low, start), (low, w))
    cut = w // 2
    top = jnp.concatenate([adj_col, fac_col[:cut]], axis=0)
    bottom = jnp.concatenate([fac_col[cut:], adjoint[w:low, left - w : left]], axis=0)
    row_block = lax.dynamic_slice(factor, (jnp.where(p == 0, low, w), 0), (w, left))
    quarter = row_quarters(row_block)
    top, bottom, quarter = lax.optimization_barrier((top, bottom, quarter))
    top, bottom = column_hops(top, bottom)
    own = row_spread(quarter)
    up = lax.ppermute(own, ROW, ring_pairs(1))
    down = lax.ppermute(own, ROW, ring_pairs(-1))
    top, bottom, up, down = lax.optimization_barrier((top, bottom, up, down))
    even_top, odd_top = column_swap(top)
    even_bottom, odd_bottom = column_swap(bottom)
    terms, a0, l1_below = sums(
        even_top, even_bottom, odd_top, odd_bottom, inverse[0], factor
    )
    across_first = lax.ppermute(up[0], ROW, ring_pairs(1))
    across_second = lax.ppermute(down[1], ROW, ring_pairs(-1))
    terms, across_first, across_second = lax.optimization_barrier((terms, across_first, across_second))
    terms = lax.all_to_all(terms, ROW, 0, 0)
    diag_t, inverse_t, base = invert(inverse, adjoint, a0)

    r31 = gather_corner(own, down, up, across_first)
    last = lax.axis_size(COL) - 1
    near = lax.ppermute(r31, COL, [(last, last - 2)])
    far = lax.ppermute(r31, COL, [(last, 1)])
    across = lax.ppermute(r31, COL, [(last, last - 4)])
    r31 = jnp.where(q == last - 2, near, jnp.where(q == 1, far, jnp.where(q == last - 4, across, r31)))
    r31 = jnp.where(q % 2 == 1, r31, lax.ppermute(r31, COL, [(i, i - 1) for i in range(1, last + 1, 2)]))
    terms, diag_t, inverse_t, base = lax.optimization_barrier((terms, diag_t, inverse_t, base))
    shares, small = middle(terms, r31, inverse[1])
    small = lax.all_to_all(small, ROW, 0, 0)
    base, r_high, r_low = trail(
        adjoint, base, a0, l1_below, inverse[1], r31, own, down, up, across_first, across_second
    )
    small, shares, base, r_high, r_low = lax.optimization_barrier((small, shares, base, r_high, r_low))
    shares = lax.all_to_all(shares, ROW, 0, 0)
    count = lax.axis_size(COL)
    before, after, across = (
        lax.ppermute(small, COL, [(i, (i + step) % count) for i in range(count)]) for step in (2, -2, 4)
    )
    theirs = lax.ppermute(
        jnp.stack([small, after, across, before]), COL, [(i, i ^ 1) for i in range(count)]
    )
    lhs, corner, diag = chain(
        small, before, after, across, theirs, inverse, inverse_t, diag_t, odd_bottom[low - cut :], r31
    )
    return final(base, shares, lhs, corner, diag, r_high, r_low)


def solution(mesh):
    return jax.shard_map(
        per_device,
        mesh=mesh,
        in_specs=(P(ROW, COL), P(ROW, COL), P()),
        out_specs=P(ROW, COL),
        check_vma=False,
    )
```

```python
import functools

import jax
import jax.numpy as jnp
from jax import lax
from jax.experimental import pallas as pl
from jax.experimental.pallas import tpu as pltpu
from jax.sharding import PartitionSpec as P

ROW = "row"
COL = "col"
RING = 4
VMEM = pl.BlockSpec(memory_space=pltpu.VMEM)
HBM = pl.BlockSpec(memory_space=pltpu.HBM)


def product(left, right):
    return jnp.dot(left, right, precision=lax.Precision.HIGHEST, preferred_element_type=jnp.float32)


def split(value):
    high = value.astype(jnp.bfloat16)
    return high, (value - high.astype(jnp.float32)).astype(jnp.bfloat16)


def product_split(left, right_high, right_low):
    left_high, left_low = split(left)
    dot = functools.partial(jnp.dot, preferred_element_type=jnp.float32)
    return dot(left_high, right_high) + (dot(left_low, right_high) + dot(left_high, right_low))


def masks(width):
    rows = lax.broadcasted_iota(jnp.int32, (width, width), 0)
    cols = lax.broadcasted_iota(jnp.int32, (width, width), 1)
    return rows > cols, rows == cols


def tril(matrix):
    below, diag = masks(matrix.shape[0])
    return jnp.where(below | diag, matrix, 0.0)


def halved_lower(matrix):
    below, diag = masks(matrix.shape[0])
    return jnp.where(below, matrix, jnp.where(diag, 0.5 * matrix, 0.0))


def params(megabytes):
    return pltpu.CompilerParams(vmem_limit_bytes=megabytes << 20)


def cost(flops, bytes_accessed):
    return pl.CostEstimate(flops=flops, bytes_accessed=bytes_accessed, transcendentals=0)


def in_hbm(value):
    return pltpu.with_memory_space_constraint(value, pltpu.HBM)


def tile_shape(*shape):
    return jax.ShapeDtypeStruct(shape, jnp.float32)


def invert_kernel(tiles, adj, a0, out, out_t, base, power, total, held, sems):
    width = tiles.shape[-1]
    low, left = 2 * width, 4 * width
    q = lax.axis_index(COL)
    half = low // 2
    keep = [(slice(i * half, (i + 1) * half), slice(0, adj.shape[1])) for i in range(2)]
    keep += [(slice(low + i * half, low + (i + 1) * half), slice(left, adj.shape[1])) for i in range(2)]
    stage = [held.at[i, :, slice(0, at[1].stop - at[1].start)] for i, at in enumerate(keep)]
    loads = [pltpu.make_async_copy(adj.at[at], dst, sems.at[i]) for i, (at, dst) in enumerate(zip(keep, stage))]
    stores = [pltpu.make_async_copy(src, base.at[at], sems.at[i + 4]) for i, (at, src) in enumerate(zip(keep, stage))]
    for load in loads:
        load.start()
    below, diag = masks(width)
    scales = []
    for j in range(2):
        tile = tiles[j]
        out_t[j] = tile.T
        only = jnp.where(diag, tile, 0.0)
        power[j] = jnp.where(below, tile / jnp.sum(only, axis=1, keepdims=True), 0.0)
        total[j] = jnp.where(diag, 1.0, 0.0) - power[j]
        scales.append(1.0 / jnp.sum(only, axis=0, keepdims=True))

    for load in loads:
        load.wait()

    @pl.when(q == 0)
    def _():
        for i in range(2):
            held[2 + i, :, :width] = a0[i * half : (i + 1) * half, :]

    for store in stores:
        store.start()

    @pl.loop(0, (width - 1).bit_length() - 1)
    def _(step):
        for j in range(2):
            power[j] = product(power[j], power[j])
        for j in range(2):
            total[j] = total[j] + product(total[j], power[j])

    for j in range(2):
        out[j] = (total[j] * scales[j]).T
    for store in stores:
        store.wait()


def invert(tiles, adjoint, a0):
    w = tiles.shape[-1]
    return pl.pallas_call(
        invert_kernel,
        out_shape=(pltpu.HBM((2, w, w), jnp.float32),) * 2 + (pltpu.HBM(adjoint.shape, jnp.float32),),
        in_specs=[VMEM, HBM, VMEM],
        out_specs=(VMEM,) * 2 + (HBM,),
        scratch_shapes=[pltpu.VMEM((2, w, w), jnp.float32)] * 2
        + [pltpu.VMEM((4, w, adjoint.shape[1]), jnp.float32), pltpu.SemaphoreType.DMA((8,))],
        compiler_params=params(14),
        cost_estimate=cost(28 * 12 * w**3, 1 << 20),
        name="invert",
    )(tiles, in_hbm(adjoint), in_hbm(a0))


def rows_kernel(own, down, up, across_first, across_second, corner, r_high, r_low, held, sems):
    w = corner.shape[0]
    left = own.shape[-1]
    quarter = w // RING
    z = lax.axis_index(ROW) // RING
    sources = [own.at[0], down.at[0], across_first, up.at[0], own.at[1], down.at[1], across_second, up.at[1]]
    fetches = [pltpu.make_async_copy(src, held.at[k], sems.at[k]) for k, src in enumerate(sources)]
    for fetch in fetches:
        fetch.start()
    for k, fetch in enumerate(fetches):
        fetch.wait()
        place = pl.multiple_of(lax.rem(z + k, RING) * quarter, quarter)
        high, low = split(held[k])
        target = pl.ds(k // RING * w + place, quarter)
        r_high[target, :] = high
        r_low[target, :] = low
        if k < RING:
            corner[pl.ds(place, quarter), :] = held[k, :, left - w :]


def gather_rows(*pieces):
    shape = pieces[0].shape
    w, left = shape[1] * RING, shape[2]
    panel = pltpu.HBM((2 * w, left), jnp.bfloat16)
    return pl.pallas_call(
        rows_kernel,
        out_shape=(tile_shape(w, w), panel, panel),
        in_specs=[HBM] * len(pieces),
        out_specs=(VMEM,) * 3,
        scratch_shapes=[
            pltpu.VMEM((2 * RING, shape[1], left), jnp.float32),
            pltpu.SemaphoreType.DMA((2 * RING,)),
        ],
        compiler_params=params(8),
        cost_estimate=cost(1 << 10, 1 << 19),
        name="rows",
    )(*[in_hbm(value) for value in pieces])


def small_rows(w, rows):
    return -(-3 * (w // lax.axis_size(COL) // rows) // 8) * 8


def sums_kernel(even_top, even_bottom, odd_top, odd_bottom, inv0, factor, out, a0_out, l1_out, high, low, small, tall):
    step = pl.program_id(0)
    w = inv0.shape[0]
    rows = lax.axis_size(ROW)
    first = lax.axis_index(ROW) == 0
    per_step = w // (w * 4 // rows)
    cols = 4 * w // rows
    piece = small.shape[1] // rows

    @pl.when(step == 0)
    def _():
        cut = w // 2
        l0, l1 = even_top[: 2 * w], odd_top[: 2 * w]
        c0 = jnp.concatenate([even_top[2 * w :], even_bottom[: 2 * w - cut]], axis=0)
        c1 = jnp.concatenate([odd_top[2 * w :], odd_bottom[: 2 * w - cut]], axis=0)
        skip = first & (lax.broadcasted_iota(jnp.int32, l0.shape, 0) < w)
        a0 = jnp.where(skip, 0.0, product(l0, inv0[...]))
        below = jnp.where(skip, 0.0, l1)
        a0_out[...] = a0
        l1_out[...] = below
        high[:, :w], low[:, :w] = split(a0)
        high[:, w:], low[:, w:] = split(below)
        tall[0] = a0.T
        tall[1] = below.T
        share = w // lax.axis_size(COL)
        mine = pl.ds(pl.multiple_of(lax.axis_index(COL) * share, share), share)
        diag_below = jnp.where(skip, 0.0, c0)
        next_below = jnp.where(skip, 0.0, c1)
        raw_next = jnp.where(first, l1[:w], 0.0)
        tall[2, :, :w] = c1[:w].T
        small[0] = jnp.where(first, even_top[mine, :], 0.0) - product(tall[0, mine, :], diag_below)
        small[1] = jnp.where(first, odd_top[mine, :], 0.0) - product(tall[0, mine, :], next_below)
        small[2] = product(tall[1, mine, :], next_below) - product(tall[2, mine, :w], raw_next)

    part = product_split(factor[...].T, high[...], low[...])
    out[:, :cols, :] = part[:, :w].reshape(per_step, cols, w)
    out[:, cols : 2 * cols, :] = part[:, w:].reshape(per_step, cols, w)
    lines = per_step * piece
    for j in range(3):
        part = small[j, pl.ds(pl.multiple_of(step * lines, lines), lines), :]
        at = 2 * cols + j * piece
        out[:, at : at + piece, :] = part.reshape(per_step, piece, w)
    at = 2 * cols + 3 * piece
    out[:, at:, :] = jnp.zeros((per_step, out.shape[1] - at, w), jnp.float32)


def sums(even_top, even_bottom, odd_top, odd_bottom, inv0, factor):
    w = inv0.shape[0]
    rows = lax.axis_size(ROW)
    share = w // lax.axis_size(COL)
    height = 2 * (4 * w // rows) + small_rows(w, rows)
    const = lambda i: (0, 0)
    whole = lambda value: pl.BlockSpec(value.shape, const, pipeline_mode=pl.Buffered(1))
    return pl.pallas_call(
        sums_kernel,
        grid=(4,),
        out_shape=(pltpu.HBM((rows, height, w), jnp.float32),)
        + (pltpu.HBM((2 * w, w), jnp.float32),) * 2,
        in_specs=[whole(even_top), whole(even_bottom), whole(odd_top), whole(odd_bottom), whole(inv0)]
        + [pl.BlockSpec((2 * w, w), lambda i: (1, i))],
        out_specs=(
            pl.BlockSpec((rows // 4, height, w), lambda i: (i, 0, 0)),
            pl.BlockSpec((2 * w, w), const),
            pl.BlockSpec((2 * w, w), const),
        ),
        scratch_shapes=[
            pltpu.VMEM((2 * w, 2 * w), jnp.bfloat16),
            pltpu.VMEM((2 * w, 2 * w), jnp.bfloat16),
            pltpu.VMEM((3, share, w), jnp.float32),
            pltpu.VMEM((3, w, 2 * w), jnp.float32),
        ],
        compiler_params=params(14),
        cost_estimate=cost(4 << 30, 8 << 20),
        name="sums",
    )(even_top, even_bottom, odd_top, odd_bottom, inv0, in_hbm(factor))


def middle_kernel(terms, r31, inv1, out, out_small, r31_v, inv1_v, out_v, small_v, sems):
    rows, cols = out.shape[:2]
    fetches = [
        pltpu.make_async_copy(r31, r31_v, sems.at[0]),
        pltpu.make_async_copy(inv1, inv1_v, sems.at[1]),
    ]
    for fetch in fetches:
        fetch.start()
    small = terms[0, 2 * cols :, :]
    for i in range(1, rows):
        small = small + terms[i, 2 * cols :, :]
    for i in range(rows):
        small_v[i] = small
    stores = [pltpu.make_async_copy(small_v, out_small, sems.at[2])]
    stores[0].start()
    total = terms[0, : 2 * cols, :]
    for i in range(1, rows):
        total = total + terms[i, : 2 * cols, :]
    top = total[:cols]
    for fetch in fetches:
        fetch.wait()
    out_v[0] = top
    out_v[1] = product(total[cols:] - product(top, r31_v[...]), inv1_v[...])
    stores += [pltpu.make_async_copy(out_v.at[min(i, 1)], out.at[i], sems.at[3 + i]) for i in range(rows)]
    for store in stores[1:]:
        store.start()
    for store in stores:
        store.wait()


def middle(terms, r31, inv1):
    rows, height, w = terms.shape
    small = small_rows(w, rows)
    cols = (height - small) // 2
    return pl.pallas_call(
        middle_kernel,
        out_shape=(pltpu.HBM((rows, cols, w), jnp.float32), pltpu.HBM((rows, small, w), jnp.float32)),
        in_specs=[VMEM, HBM, HBM],
        out_specs=(HBM, HBM),
        scratch_shapes=[
            pltpu.VMEM((w, w), jnp.float32),
            pltpu.VMEM((w, w), jnp.float32),
            pltpu.VMEM((2, cols, w), jnp.float32),
            pltpu.VMEM((rows, small, w), jnp.float32),
            pltpu.SemaphoreType.DMA((3 + rows,)),
        ],
        compiler_params=params(10),
        cost_estimate=cost(1 << 28, 6 << 20),
        name="middle",
    )(terms, in_hbm(r31), in_hbm(inv1))


def trail_kernel(adj, a0, l1, inv1, r31, r_high, r_low, base, out, small):
    w = inv1.shape[0]
    left = 4 * w
    q = lax.axis_index(COL)
    last_q = lax.axis_size(COL) - 1

    @pl.when(pl.program_id(0) == 0)
    def _():
        small[0], small[1] = split(inv1[...])
        small[2], small[3] = split(product(r31[...], inv1[...]))

    first = a0[...]
    second = product_split(l1[...], small[0], small[1]) - product_split(first, small[2], small[3])
    lhs = jnp.concatenate([first, second], axis=1)
    out[...] = adj[...] - product_split(lhs, r_high[...], r_low[...])

    @pl.when(q == last_q)
    def _():
        out[:, left - w :] = second


def trail(adjoint, base, a0, l1, inv1, r31, r_high, r_low):
    rows, cols = adjoint.shape
    w = inv1.shape[0]
    steps = 2
    blk = rows // 2 // steps
    low = lambda i: (i, 0)
    block = lambda i: (steps + i, 0)
    whole = lambda value: pl.BlockSpec(value.shape, lambda i: (0, 0), pipeline_mode=pl.Buffered(1))
    return pl.pallas_call(
        trail_kernel,
        grid=(steps,),
        out_shape=pltpu.HBM(adjoint.shape, jnp.float32),
        in_specs=[
            pl.BlockSpec((blk, 4 * w), block),
            pl.BlockSpec((blk, w), low),
            pl.BlockSpec((blk, w), low),
            whole(inv1),
            whole(r31),
            whole(r_high),
            whole(r_low),
            HBM,
        ],
        out_specs=pl.BlockSpec((blk, 4 * w), block),
        scratch_shapes=[pltpu.VMEM((4, w, w), jnp.bfloat16)],
        input_output_aliases={7: 0},
        compiler_params=params(16),
        cost_estimate=cost(4 << 30, 10 << 20),
        name="trail",
    )(*[in_hbm(value) for value in (adjoint, a0, l1, inv1, r31, r_high, r_low, base)])


def chain_kernel(
    mine, before, after, across, theirs, inverse, inverse_t, diag_t, diag31, r31, lhs, corner, diag, tiles
):
    w = inverse.shape[-1]
    rows = mine.shape[0]
    p = lax.axis_index(ROW)
    q = lax.axis_index(COL)
    share = w // lax.axis_size(COL)
    piece = share // rows

    @pl.when((p == 0) | (p == rows - 1))
    def _():
        core = lax.rem(q, 2)
        for k, shared in ((0, mine), (1, after), (2, across), (3, before)):
            chip = lax.rem(q // 2 + k, RING)
            for other in range(2):
                at = chip * 2 + (1 - core if other else core)
                target = pl.ds(pl.multiple_of(at * share, share), share)
                for j in range(3):
                    lines = slice(j * piece, (j + 1) * piece)
                    value = theirs[k, :, lines, :] if other else shared[:, lines, :]
                    tiles[j, target, :] = value.reshape(share, w)
        t01, x11 = tiles[1], tiles[2]

        def adjoint_diag(j, dprime):
            inner = halved_lower(product(diag_t[j], tril(dprime)))
            wmat = product(product(inverse_t[j], inner), inverse[j])
            return wmat + wmat.T

        known = r31[...]
        side = product(inverse_t[1], x11 + product(known.T, t01))
        g0 = adjoint_diag(0, tiles[0])
        a132 = product(t01 - product(g0, known), inverse[1])
        diag[...] = halved_lower(g0)

        @pl.when(p == 0)
        def _():
            lhs[:, :w] = g0
            lhs[:, w:] = a132
            corner[...] = a132

        @pl.when(p != 0)
        def _():
            a132_t = a132.T
            g1 = adjoint_diag(1, diag31[...] - side - product(a132_t, known))
            lhs[:, :w] = a132_t
            lhs[:, w:] = g1
            corner[...] = halved_lower(g1)


def chain(*operands):
    w = operands[5].shape[-1]
    return pl.pallas_call(
        chain_kernel,
        out_shape=tuple(pltpu.HBM((w, n * w), jnp.float32) for n in (2, 1, 1)),
        in_specs=[VMEM] * len(operands),
        out_specs=(VMEM,) * 3,
        scratch_shapes=[pltpu.VMEM((3, w, w), jnp.float32)],
        compiler_params=params(14),
        cost_estimate=cost(1 << 20, 1 << 10),
        name="chain",
    )(*operands)


def final_kernel(base, got, lhs, corner, diag, r_high, r_low, out, *scratch):
    got_v, lhs_v, corner_v, diag_v, r_high_v, r_low_v, rows_buf, sems = scratch
    rows, cols, w = got.shape
    left = 4 * w
    p = lax.axis_index(ROW)
    q = lax.axis_index(COL)
    last_q = lax.axis_size(COL) - 1

    @pl.when((p == 0) | (p == rows - 1))
    def _():
        start = jnp.where(p == 0, 2 * w, w)
        region = (pl.ds(start, w), pl.ds(0, left))
        moves = [
            (lhs, lhs_v),
            (r_high, r_high_v),
            (r_low, r_low_v),
            (base.at[region], rows_buf),
            (got, got_v),
            (corner, corner_v),
            (diag, diag_v),
        ]
        fetches = [pltpu.make_async_copy(src, dst, sems.at[i]) for i, (src, dst) in enumerate(moves)]
        for fetch in fetches:
            fetch.start()
        for fetch in fetches:
            fetch.wait()
        stores = []
        for j in range(4):
            at = slice(j * w, (j + 1) * w)
            piece = rows // 4
            value = rows_buf[:, at] - got_v[j * piece : (j + 1) * piece].reshape(w, w).T
            rows_buf[:, at] = value - product_split(lhs_v[...], r_high_v[:, at], r_low_v[:, at])
            if j == 3:

                @pl.when(q == last_q)
                def _():
                    rows_buf[:, at] = corner_v[...]

            stores.append(
                pltpu.make_async_copy(
                    rows_buf.at[:, at], out.at[pl.ds(start, w), at], sems.at[len(moves) + j]
                )
            )
            stores[-1].start()

        @pl.when((p == 0) & (q == 0))
        def _():
            store = pltpu.make_async_copy(
                diag_v, out.at[pl.ds(2 * w, w), pl.ds(left, w)], sems.at[len(moves) + 4]
            )
            store.start()
            store.wait()

        for store in stores:
            store.wait()


def final(base, *operands):
    w = operands[1].shape[0]
    return pl.pallas_call(
        final_kernel,
        out_shape=tile_shape(*base.shape),
        in_specs=[HBM] * (1 + len(operands)),
        out_specs=HBM,
        scratch_shapes=[
            pltpu.VMEM(operands[i].shape, operands[i].dtype) for i in range(len(operands))
        ]
        + [pltpu.VMEM((w, 4 * w), jnp.float32), pltpu.SemaphoreType.DMA((12,))],
        input_output_aliases={0: 0},
        compiler_params=params(16),
        cost_estimate=cost(2 << 30, 8 << 20),
        name="final",
    )(base, *[in_hbm(value) for value in operands])


def column_hops(top, bottom):
    q = lax.axis_index(COL)
    last = lax.axis_size(COL) - 1
    near, far = [(0, 2), (last, last - 2)], [(0, last - 1), (last, 1)]
    near_top = lax.ppermute(top, COL, near)
    far_bottom = lax.ppermute(bottom, COL, far)
    near_bottom = lax.ppermute(bottom, COL, near)
    far_top = lax.ppermute(top, COL, far)
    upper = lax.ppermute(near_top, COL, [(2, 4), (last - 2, last - 4)])
    lower = lax.ppermute(far_bottom, COL, [(last - 1, 4), (1, last - 4)])

    def choose(own, near_value, far_value, across):
        value = jnp.where((q == 1) | (q == last - 1), far_value, across)
        value = jnp.where((q == 2) | (q == last - 2), near_value, value)
        return jnp.where((q == 0) | (q == last), own, value)

    return choose(top, near_top, far_top, upper), choose(bottom, near_bottom, far_bottom, lower)


def column_swap(mine):
    theirs = lax.ppermute(mine, COL, [(i, i ^ 1) for i in range(lax.axis_size(COL))])
    even = lax.axis_index(COL) % 2 == 0
    return jnp.where(even, mine, theirs), jnp.where(even, theirs, mine)


def row_quarters(block):
    p = lax.axis_index(ROW)
    last = lax.axis_size(ROW) - 1
    top = RING - 1
    quarters = block.reshape(RING, -1, block.shape[1])
    first = p == 0
    near = lax.ppermute(
        jnp.where(first, quarters[1], quarters[top - 1]), ROW, [(0, RING), (last, last - RING)]
    )
    far = lax.ppermute(jnp.where(first, quarters[top], quarters[0]), ROW, [(0, last - top), (last, top)])
    across = lax.ppermute(
        jnp.where(first, quarters[2], quarters[1]), ROW, [(0, 2 * RING), (last, last - 2 * RING)]
    )
    mine = jnp.where(first, quarters[0], quarters[top])
    mine = jnp.where((p == RING) | (p == last - RING), near, mine)
    mine = jnp.where((p == last - top) | (p == top), far, mine)
    return jnp.where((p == 2 * RING) | (p == last - 2 * RING), across, mine)


def row_spread(mine):
    top = RING - 1
    x = lax.axis_index(ROW) % RING
    lines = range(0, lax.axis_size(ROW), RING)
    near = lax.ppermute(mine, ROW, [e for s in lines for e in ((s, s + 1), (s + top, s + top - 1))])
    far = lax.ppermute(mine, ROW, [e for s in lines for e in ((s, s + top), (s + top, s))])
    across = lax.ppermute(mine, ROW, [e for s in lines for e in ((s, s + 2), (s + top, s + top - 2))])
    from_first = jnp.where(x == 0, mine, jnp.where(x == 1, near, jnp.where(x == 2, across, far)))
    from_last = jnp.where(x == top, mine, jnp.where(x == 2, near, jnp.where(x == 1, across, far)))
    return jnp.stack([from_first, from_last])


def ring_pairs(step):
    count = lax.axis_size(ROW)
    return [(i, (i + step * RING) % count) for i in range(count)]


def per_device(factor, adjoint, inverse):
    w = inverse.shape[-1]
    rows = lax.axis_size(ROW)
    p = lax.axis_index(ROW)
    q = lax.axis_index(COL)
    low, left = 2 * w, 4 * w

    start = jnp.where(q == 0, left, left - w)
    adj_col = lax.dynamic_slice(adjoint, (low, start), (low, w))
    fac_col = lax.dynamic_slice(factor, (low, start), (low, w))
    cut = w // 2
    top = jnp.concatenate([adj_col, fac_col[:cut]], axis=0)
    bottom = jnp.concatenate([fac_col[cut:], adjoint[w:low, left - w : left]], axis=0)
    row_block = lax.dynamic_slice(factor, (jnp.where(p == 0, low, w), 0), (w, left))
    quarter = row_quarters(row_block)
    top, bottom, quarter = lax.optimization_barrier((top, bottom, quarter))
    top, bottom = column_hops(top, bottom)
    own = row_spread(quarter)
    up = lax.ppermute(own, ROW, ring_pairs(1))
    down = lax.ppermute(own, ROW, ring_pairs(-1))
    even_top, odd_top = column_swap(top)
    even_bottom, odd_bottom = column_swap(bottom)
    terms, a0, l1_below = sums(
        even_top, even_bottom, odd_top, odd_bottom, inverse[0], factor
    )
    across_first = lax.ppermute(up[0], ROW, ring_pairs(1))
    across_second = lax.ppermute(down[1], ROW, ring_pairs(-1))
    terms, across_first, across_second = lax.optimization_barrier((terms, across_first, across_second))
    terms = lax.all_to_all(terms, ROW, 0, 0)
    diag_t, inverse_t, base = invert(inverse, adjoint, a0)

    r31, r_high, r_low = gather_rows(own, down, up, across_first, across_second)
    last = lax.axis_size(COL) - 1
    near = lax.ppermute(r31, COL, [(last, last - 2)])
    far = lax.ppermute(r31, COL, [(last, 1)])
    across = lax.ppermute(r31, COL, [(last, last - 4)])
    r31 = jnp.where(q == last - 2, near, jnp.where(q == 1, far, jnp.where(q == last - 4, across, r31)))
    r31 = jnp.where(q % 2 == 1, r31, lax.ppermute(r31, COL, [(i, i - 1) for i in range(1, last + 1, 2)]))
    terms, diag_t, inverse_t, base = lax.optimization_barrier((terms, diag_t, inverse_t, base))
    shares, small = middle(terms, r31, inverse[1])
    small = lax.all_to_all(small, ROW, 0, 0)
    base = trail(adjoint, base, a0, l1_below, inverse[1], r31, r_high, r_low)
    small, shares, base = lax.optimization_barrier((small, shares, base))
    shares = lax.all_to_all(shares, ROW, 0, 0)
    count = lax.axis_size(COL)
    before, after, across = (
        lax.ppermute(small, COL, [(i, (i + step) % count) for i in range(count)]) for step in (2, -2, 4)
    )
    theirs = lax.ppermute(
        jnp.stack([small, after, across, before]), COL, [(i, i ^ 1) for i in range(count)]
    )
    lhs, corner, diag = chain(
        small, before, after, across, theirs, inverse, inverse_t, diag_t, odd_bottom[low - cut :], r31
    )
    return final(base, shares, lhs, corner, diag, r_high, r_low)


def solution(mesh):
    return jax.shard_map(
        per_device,
        mesh=mesh,
        in_specs=(P(ROW, COL), P(ROW, COL), P()),
        out_specs=P(ROW, COL),
        check_vma=False,
    )
```

```python
import functools

import jax
import jax.numpy as jnp
from jax import lax
from jax.experimental import pallas as pl
from jax.experimental.pallas import tpu as pltpu
from jax.sharding import PartitionSpec as P

ROW = "row"
COL = "col"
RING = 4
VMEM = pl.BlockSpec(memory_space=pltpu.VMEM)
HBM = pl.BlockSpec(memory_space=pltpu.HBM)


def product(left, right):
    return jnp.dot(left, right, precision=lax.Precision.HIGHEST, preferred_element_type=jnp.float32)


def split(value):
    high = value.astype(jnp.bfloat16)
    return high, (value - high.astype(jnp.float32)).astype(jnp.bfloat16)


def product_split(left, right_high, right_low):
    left_high, left_low = split(left)
    dot = functools.partial(jnp.dot, preferred_element_type=jnp.float32)
    return dot(left_high, right_high) + (dot(left_low, right_high) + dot(left_high, right_low))


def masks(width):
    rows = lax.broadcasted_iota(jnp.int32, (width, width), 0)
    cols = lax.broadcasted_iota(jnp.int32, (width, width), 1)
    return rows > cols, rows == cols


def tril(matrix):
    below, diag = masks(matrix.shape[0])
    return jnp.where(below | diag, matrix, 0.0)


def halved_lower(matrix):
    below, diag = masks(matrix.shape[0])
    return jnp.where(below, matrix, jnp.where(diag, 0.5 * matrix, 0.0))


def params(megabytes):
    return pltpu.CompilerParams(vmem_limit_bytes=megabytes << 20)


def cost(flops, bytes_accessed):
    return pl.CostEstimate(flops=flops, bytes_accessed=bytes_accessed, transcendentals=0)


def in_hbm(value):
    return pltpu.with_memory_space_constraint(value, pltpu.HBM)


def tile_shape(*shape):
    return jax.ShapeDtypeStruct(shape, jnp.float32)


def invert_kernel(tiles, adj, a0, out, out_t, base, power, total, held, sems):
    width = tiles.shape[-1]
    low, left = 2 * width, 4 * width
    q = lax.axis_index(COL)
    half = low // 2
    keep = [(slice(i * half, (i + 1) * half), slice(0, adj.shape[1])) for i in range(2)]
    keep += [(slice(low + i * half, low + (i + 1) * half), slice(left, adj.shape[1])) for i in range(2)]
    stage = [held.at[i, :, slice(0, at[1].stop - at[1].start)] for i, at in enumerate(keep)]
    loads = [pltpu.make_async_copy(adj.at[at], dst, sems.at[i]) for i, (at, dst) in enumerate(zip(keep, stage))]
    stores = [pltpu.make_async_copy(src, base.at[at], sems.at[i + 4]) for i, (at, src) in enumerate(zip(keep, stage))]
    for load in loads:
        load.start()
    below, diag = masks(width)
    scales = []
    for j in range(2):
        tile = tiles[j]
        out_t[j] = tile.T
        only = jnp.where(diag, tile, 0.0)
        power[j] = jnp.where(below, tile / jnp.sum(only, axis=1, keepdims=True), 0.0)
        total[j] = jnp.where(diag, 1.0, 0.0) - power[j]
        scales.append(1.0 / jnp.sum(only, axis=0, keepdims=True))

    for load in loads:
        load.wait()

    @pl.when(q == 0)
    def _():
        for i in range(2):
            held[2 + i, :, :width] = a0[i * half : (i + 1) * half, :]

    for store in stores:
        store.start()

    @pl.loop(0, (width - 1).bit_length() - 1)
    def _(step):
        for j in range(2):
            power[j] = product(power[j], power[j])
        for j in range(2):
            total[j] = total[j] + product(total[j], power[j])

    for j in range(2):
        out[j] = (total[j] * scales[j]).T
    for store in stores:
        store.wait()


def invert(tiles, adjoint, a0):
    w = tiles.shape[-1]
    return pl.pallas_call(
        invert_kernel,
        out_shape=(pltpu.HBM((2, w, w), jnp.float32),) * 2 + (pltpu.HBM(adjoint.shape, jnp.float32),),
        in_specs=[VMEM, HBM, VMEM],
        out_specs=(VMEM,) * 2 + (HBM,),
        scratch_shapes=[pltpu.VMEM((2, w, w), jnp.float32)] * 2
        + [pltpu.VMEM((4, w, adjoint.shape[1]), jnp.float32), pltpu.SemaphoreType.DMA((8,))],
        compiler_params=params(14),
        cost_estimate=cost(28 * 12 * w**3, 1 << 20),
        name="invert",
    )(tiles, in_hbm(adjoint), in_hbm(a0))


def rows_kernel(own, down, up, across_first, across_second, corner, r_high, r_low, held, sems):
    w = corner.shape[0]
    left = own.shape[-1]
    quarter = w // RING
    z = lax.axis_index(ROW) // RING
    sources = [own.at[0], down.at[0], across_first, up.at[0], own.at[1], down.at[1], across_second, up.at[1]]
    fetches = [pltpu.make_async_copy(src, held.at[k], sems.at[k]) for k, src in enumerate(sources)]
    for fetch in fetches:
        fetch.start()
    for k, fetch in enumerate(fetches):
        fetch.wait()
        place = pl.multiple_of(lax.rem(z + k, RING) * quarter, quarter)
        high, low = split(held[k])
        target = pl.ds(k // RING * w + place, quarter)
        r_high[target, :] = high
        r_low[target, :] = low
        if k < RING:
            corner[pl.ds(place, quarter), :] = held[k, :, left - w :]


def gather_rows(*pieces):
    shape = pieces[0].shape
    w, left = shape[1] * RING, shape[2]
    panel = pltpu.HBM((2 * w, left), jnp.bfloat16)
    return pl.pallas_call(
        rows_kernel,
        out_shape=(tile_shape(w, w), panel, panel),
        in_specs=[HBM] * len(pieces),
        out_specs=(VMEM,) * 3,
        scratch_shapes=[
            pltpu.VMEM((2 * RING, shape[1], left), jnp.float32),
            pltpu.SemaphoreType.DMA((2 * RING,)),
        ],
        compiler_params=params(8),
        cost_estimate=cost(1 << 10, 1 << 19),
        name="rows",
    )(*[in_hbm(value) for value in pieces])


def small_rows(w, rows):
    return -(-3 * (w // lax.axis_size(COL) // rows) // 8) * 8


def sums_kernel(even_top, even_bottom, odd_top, odd_bottom, inv0, factor, out, a0_out, l1_out, high, low, small, tall):
    step = pl.program_id(0)
    w = inv0.shape[0]
    rows = lax.axis_size(ROW)
    first = lax.axis_index(ROW) == 0
    per_step = w // (w * 4 // rows)
    cols = 4 * w // rows
    piece = small.shape[1] // rows

    @pl.when(step == 0)
    def _():
        cut = w // 2
        l0, l1 = even_top[: 2 * w], odd_top[: 2 * w]
        c0 = jnp.concatenate([even_top[2 * w :], even_bottom[: 2 * w - cut]], axis=0)
        c1 = jnp.concatenate([odd_top[2 * w :], odd_bottom[: 2 * w - cut]], axis=0)
        skip = first & (lax.broadcasted_iota(jnp.int32, l0.shape, 0) < w)
        a0 = jnp.where(skip, 0.0, product(l0, inv0[...]))
        below = jnp.where(skip, 0.0, l1)
        a0_out[...] = a0
        l1_out[...] = below
        high[:, :w], low[:, :w] = split(a0)
        high[:, w:], low[:, w:] = split(below)
        tall[0] = a0.T
        tall[1] = below.T
        share = w // lax.axis_size(COL)
        mine = pl.ds(pl.multiple_of(lax.axis_index(COL) * share, share), share)
        diag_below = jnp.where(skip, 0.0, c0)
        next_below = jnp.where(skip, 0.0, c1)
        raw_next = jnp.where(first, l1[:w], 0.0)
        tall[2, :, :w] = c1[:w].T
        small[0] = jnp.where(first, even_top[mine, :], 0.0) - product(tall[0, mine, :], diag_below)
        small[1] = jnp.where(first, odd_top[mine, :], 0.0) - product(tall[0, mine, :], next_below)
        small[2] = product(tall[1, mine, :], next_below) - product(tall[2, mine, :w], raw_next)

    part = product_split(factor[...].T, high[...], low[...])
    out[:, :cols, :] = part[:, :w].reshape(per_step, cols, w)
    out[:, cols : 2 * cols, :] = part[:, w:].reshape(per_step, cols, w)
    lines = per_step * piece
    for j in range(3):
        part = small[j, pl.ds(pl.multiple_of(step * lines, lines), lines), :]
        at = 2 * cols + j * piece
        out[:, at : at + piece, :] = part.reshape(per_step, piece, w)
    at = 2 * cols + 3 * piece
    out[:, at:, :] = jnp.zeros((per_step, out.shape[1] - at, w), jnp.float32)


def sums(even_top, even_bottom, odd_top, odd_bottom, inv0, factor):
    w = inv0.shape[0]
    rows = lax.axis_size(ROW)
    share = w // lax.axis_size(COL)
    height = 2 * (4 * w // rows) + small_rows(w, rows)
    const = lambda i: (0, 0)
    whole = lambda value: pl.BlockSpec(value.shape, const, pipeline_mode=pl.Buffered(1))
    return pl.pallas_call(
        sums_kernel,
        grid=(4,),
        out_shape=(pltpu.HBM((rows, height, w), jnp.float32),)
        + (pltpu.HBM((2 * w, w), jnp.float32),) * 2,
        in_specs=[whole(even_top), whole(even_bottom), whole(odd_top), whole(odd_bottom), whole(inv0)]
        + [pl.BlockSpec((2 * w, w), lambda i: (1, i))],
        out_specs=(
            pl.BlockSpec((rows // 4, height, w), lambda i: (i, 0, 0)),
            pl.BlockSpec((2 * w, w), const),
            pl.BlockSpec((2 * w, w), const),
        ),
        scratch_shapes=[
            pltpu.VMEM((2 * w, 2 * w), jnp.bfloat16),
            pltpu.VMEM((2 * w, 2 * w), jnp.bfloat16),
            pltpu.VMEM((3, share, w), jnp.float32),
            pltpu.VMEM((3, w, 2 * w), jnp.float32),
        ],
        compiler_params=params(14),
        cost_estimate=cost(4 << 30, 8 << 20),
        name="sums",
    )(even_top, even_bottom, odd_top, odd_bottom, inv0, in_hbm(factor))


def middle_kernel(terms, r31, inv1, out, out_small, r31_v, inv1_v, out_v, small_v, sems):
    rows, cols = out.shape[:2]
    fetches = [
        pltpu.make_async_copy(r31, r31_v, sems.at[0]),
        pltpu.make_async_copy(inv1, inv1_v, sems.at[1]),
    ]
    for fetch in fetches:
        fetch.start()
    small = terms[0, 2 * cols :, :]
    for i in range(1, rows):
        small = small + terms[i, 2 * cols :, :]
    for i in range(rows):
        small_v[i] = small
    stores = [pltpu.make_async_copy(small_v, out_small, sems.at[2])]
    stores[0].start()
    total = terms[0, : 2 * cols, :]
    for i in range(1, rows):
        total = total + terms[i, : 2 * cols, :]
    top = total[:cols]
    for fetch in fetches:
        fetch.wait()
    out_v[0] = top
    out_v[1] = product(total[cols:] - product(top, r31_v[...]), inv1_v[...])
    stores += [pltpu.make_async_copy(out_v.at[min(i, 1)], out.at[i], sems.at[3 + i]) for i in range(rows)]
    for store in stores[1:]:
        store.start()
    for store in stores:
        store.wait()


def middle(terms, r31, inv1):
    rows, height, w = terms.shape
    small = small_rows(w, rows)
    cols = (height - small) // 2
    return pl.pallas_call(
        middle_kernel,
        out_shape=(pltpu.HBM((rows, cols, w), jnp.float32), pltpu.HBM((rows, small, w), jnp.float32)),
        in_specs=[VMEM, HBM, HBM],
        out_specs=(HBM, HBM),
        scratch_shapes=[
            pltpu.VMEM((w, w), jnp.float32),
            pltpu.VMEM((w, w), jnp.float32),
            pltpu.VMEM((2, cols, w), jnp.float32),
            pltpu.VMEM((rows, small, w), jnp.float32),
            pltpu.SemaphoreType.DMA((3 + rows,)),
        ],
        compiler_params=params(10),
        cost_estimate=cost(1 << 28, 6 << 20),
        name="middle",
    )(terms, in_hbm(r31), in_hbm(inv1))


def trail_kernel(adj, a0, l1, inv1, r31, r_high, r_low, base, out, small):
    w = inv1.shape[0]
    left = 4 * w
    q = lax.axis_index(COL)
    last_q = lax.axis_size(COL) - 1

    @pl.when(pl.program_id(0) == 0)
    def _():
        small[0], small[1] = split(inv1[...])
        small[2], small[3] = split(product(r31[...], inv1[...]))

    first = a0[...]
    second = product_split(l1[...], small[0], small[1]) - product_split(first, small[2], small[3])
    lhs = jnp.concatenate([first, second], axis=1)
    out[...] = adj[...] - product_split(lhs, r_high[...], r_low[...])

    @pl.when(q == last_q)
    def _():
        out[:, left - w :] = second


def trail(adjoint, base, a0, l1, inv1, r31, r_high, r_low):
    rows, cols = adjoint.shape
    w = inv1.shape[0]
    steps = 2
    blk = rows // 2 // steps
    low = lambda i: (i, 0)
    block = lambda i: (steps + i, 0)
    whole = lambda value: pl.BlockSpec(value.shape, lambda i: (0, 0), pipeline_mode=pl.Buffered(1))
    return pl.pallas_call(
        trail_kernel,
        grid=(steps,),
        out_shape=pltpu.HBM(adjoint.shape, jnp.float32),
        in_specs=[
            pl.BlockSpec((blk, 4 * w), block),
            pl.BlockSpec((blk, w), low),
            pl.BlockSpec((blk, w), low),
            whole(inv1),
            whole(r31),
            whole(r_high),
            whole(r_low),
            HBM,
        ],
        out_specs=pl.BlockSpec((blk, 4 * w), block),
        scratch_shapes=[pltpu.VMEM((4, w, w), jnp.bfloat16)],
        input_output_aliases={7: 0},
        compiler_params=params(16),
        cost_estimate=cost(4 << 30, 10 << 20),
        name="trail",
    )(*[in_hbm(value) for value in (adjoint, a0, l1, inv1, r31, r_high, r_low, base)])


def chain_kernel(
    mine, before, after, across, theirs, inverse, inverse_t, diag_t, diag31, r31, r_high, r_low, base, out,
    tiles, lhs, diag, r_high_v, r_low_v, rows_buf, sems
):
    w = inverse.shape[-1]
    rows = mine.shape[0]
    p = lax.axis_index(ROW)
    q = lax.axis_index(COL)
    share = w // lax.axis_size(COL)
    piece = share // rows

    @pl.when((p == 0) | (p == rows - 1))
    def _():
        left = 4 * w
        start = jnp.where(p == 0, 2 * w, w)
        region = (pl.ds(start, w), pl.ds(0, left))
        fetches = [
            pltpu.make_async_copy(r_high, r_high_v, sems.at[0]),
            pltpu.make_async_copy(r_low, r_low_v, sems.at[1]),
            pltpu.make_async_copy(base.at[region], rows_buf, sems.at[2]),
        ]
        for fetch in fetches:
            fetch.start()
        core = lax.rem(q, 2)
        for k, shared in ((0, mine), (1, after), (2, across), (3, before)):
            chip = lax.rem(q // 2 + k, RING)
            for other in range(2):
                at = chip * 2 + (1 - core if other else core)
                target = pl.ds(pl.multiple_of(at * share, share), share)
                for j in range(3):
                    lines = slice(j * piece, (j + 1) * piece)
                    value = theirs[k, :, lines, :] if other else shared[:, lines, :]
                    tiles[j, target, :] = value.reshape(share, w)
        t01, x11 = tiles[1], tiles[2]

        def adjoint_diag(j, dprime):
            inner = halved_lower(product(diag_t[j], tril(dprime)))
            wmat = product(product(inverse_t[j], inner), inverse[j])
            return wmat + wmat.T

        known = r31[...]
        side = product(inverse_t[1], x11 + product(known.T, t01))
        g0 = adjoint_diag(0, tiles[0])
        a132 = product(t01 - product(g0, known), inverse[1])
        for fetch in fetches:
            fetch.wait()

        def update(corner):
            rows_buf[...] = rows_buf[...] - product_split(lhs[...], r_high_v[...], r_low_v[...])

            @pl.when(q == lax.axis_size(COL) - 1)
            def _():
                rows_buf[:, left - w :] = corner

            store = pltpu.make_async_copy(rows_buf, out.at[region], sems.at[3])
            store.start()
            store.wait()

        @pl.when(p == 0)
        def _():
            lhs[:, :w] = g0
            lhs[:, w:] = a132
            update(a132)

            @pl.when(q == 0)
            def _():
                diag[...] = halved_lower(g0)
                store = pltpu.make_async_copy(
                    diag, out.at[pl.ds(2 * w, w), pl.ds(left, w)], sems.at[4]
                )
                store.start()
                store.wait()

        @pl.when(p != 0)
        def _():
            a132_t = a132.T
            g1 = adjoint_diag(1, diag31[...] - side - product(a132_t, known))
            lhs[:, :w] = a132_t
            lhs[:, w:] = g1
            update(halved_lower(g1))


def chain(*operands):
    w = operands[5].shape[-1]
    base = operands[-1]
    panel = pltpu.VMEM((2 * w, 4 * w), jnp.bfloat16)
    return pl.pallas_call(
        chain_kernel,
        out_shape=pltpu.HBM(base.shape, jnp.float32),
        in_specs=[VMEM] * (len(operands) - 3) + [HBM] * 3,
        out_specs=HBM,
        scratch_shapes=[
            pltpu.VMEM((3, w, w), jnp.float32),
            pltpu.VMEM((w, 2 * w), jnp.float32),
            pltpu.VMEM((w, w), jnp.float32),
            panel,
            panel,
            pltpu.VMEM((w, 4 * w), jnp.float32),
            pltpu.SemaphoreType.DMA((5,)),
        ],
        input_output_aliases={len(operands) - 1: 0},
        compiler_params=params(18),
        cost_estimate=cost(1 << 20, 1 << 10),
        name="chain",
    )(*operands[:-3], *[in_hbm(value) for value in operands[-3:]])


def final_kernel(base, got, out, got_v, rows_buf, sems):
    rows, cols, w = got.shape
    left = 4 * w
    p = lax.axis_index(ROW)
    q = lax.axis_index(COL)
    last_q = lax.axis_size(COL) - 1

    @pl.when((p == 0) | (p == rows - 1))
    def _():
        start = jnp.where(p == 0, 2 * w, w)
        region = (pl.ds(start, w), pl.ds(0, left))
        fetches = [
            pltpu.make_async_copy(base.at[region], rows_buf, sems.at[0]),
            pltpu.make_async_copy(got, got_v, sems.at[1]),
        ]
        for fetch in fetches:
            fetch.start()
        for fetch in fetches:
            fetch.wait()
        stores = []
        piece = rows // 4
        for j in range(4):
            at = slice(j * w, (j + 1) * w)
            value = rows_buf[:, at] - got_v[j * piece : (j + 1) * piece].reshape(w, w).T
            if j == 3:
                value = jnp.where(q == last_q, rows_buf[:, at], value)
            rows_buf[:, at] = value
            stores.append(
                pltpu.make_async_copy(rows_buf.at[:, at], out.at[pl.ds(start, w), at], sems.at[2 + j])
            )
            stores[-1].start()
        for store in stores:
            store.wait()


def final(base, got):
    w = got.shape[2]
    return pl.pallas_call(
        final_kernel,
        out_shape=tile_shape(*base.shape),
        in_specs=[HBM] * 2,
        out_specs=HBM,
        scratch_shapes=[
            pltpu.VMEM(got.shape, jnp.float32),
            pltpu.VMEM((w, 4 * w), jnp.float32),
            pltpu.SemaphoreType.DMA((6,)),
        ],
        input_output_aliases={0: 0},
        compiler_params=params(8),
        cost_estimate=cost(1 << 20, 4 << 20),
        name="final",
    )(in_hbm(base), in_hbm(got))


def column_hops(top, bottom):
    q = lax.axis_index(COL)
    last = lax.axis_size(COL) - 1
    near, far = [(0, 2), (last, last - 2)], [(0, last - 1), (last, 1)]
    near_top = lax.ppermute(top, COL, near)
    far_bottom = lax.ppermute(bottom, COL, far)
    near_bottom = lax.ppermute(bottom, COL, near)
    far_top = lax.ppermute(top, COL, far)
    upper = lax.ppermute(near_top, COL, [(2, 4), (last - 2, last - 4)])
    lower = lax.ppermute(far_bottom, COL, [(last - 1, 4), (1, last - 4)])

    def choose(own, near_value, far_value, across):
        value = jnp.where((q == 1) | (q == last - 1), far_value, across)
        value = jnp.where((q == 2) | (q == last - 2), near_value, value)
        return jnp.where((q == 0) | (q == last), own, value)

    return choose(top, near_top, far_top, upper), choose(bottom, near_bottom, far_bottom, lower)


def column_swap(mine):
    theirs = lax.ppermute(mine, COL, [(i, i ^ 1) for i in range(lax.axis_size(COL))])
    even = lax.axis_index(COL) % 2 == 0
    return jnp.where(even, mine, theirs), jnp.where(even, theirs, mine)


def row_quarters(block):
    p = lax.axis_index(ROW)
    last = lax.axis_size(ROW) - 1
    top = RING - 1
    quarters = block.reshape(RING, -1, block.shape[1])
    first = p == 0
    near = lax.ppermute(
        jnp.where(first, quarters[1], quarters[top - 1]), ROW, [(0, RING), (last, last - RING)]
    )
    far = lax.ppermute(jnp.where(first, quarters[top], quarters[0]), ROW, [(0, last - top), (last, top)])
    across = lax.ppermute(
        jnp.where(first, quarters[2], quarters[1]), ROW, [(0, 2 * RING), (last, last - 2 * RING)]
    )
    mine = jnp.where(first, quarters[0], quarters[top])
    mine = jnp.where((p == RING) | (p == last - RING), near, mine)
    mine = jnp.where((p == last - top) | (p == top), far, mine)
    return jnp.where((p == 2 * RING) | (p == last - 2 * RING), across, mine)


def row_spread(mine):
    top = RING - 1
    x = lax.axis_index(ROW) % RING
    lines = range(0, lax.axis_size(ROW), RING)
    near = lax.ppermute(mine, ROW, [e for s in lines for e in ((s, s + 1), (s + top, s + top - 1))])
    far = lax.ppermute(mine, ROW, [e for s in lines for e in ((s, s + top), (s + top, s))])
    across = lax.ppermute(mine, ROW, [e for s in lines for e in ((s, s + 2), (s + top, s + top - 2))])
    from_first = jnp.where(x == 0, mine, jnp.where(x == 1, near, jnp.where(x == 2, across, far)))
    from_last = jnp.where(x == top, mine, jnp.where(x == 2, near, jnp.where(x == 1, across, far)))
    return jnp.stack([from_first, from_last])


def ring_pairs(step):
    count = lax.axis_size(ROW)
    return [(i, (i + step * RING) % count) for i in range(count)]


def per_device(factor, adjoint, inverse):
    w = inverse.shape[-1]
    rows = lax.axis_size(ROW)
    p = lax.axis_index(ROW)
    q = lax.axis_index(COL)
    low, left = 2 * w, 4 * w

    start = jnp.where(q == 0, left, left - w)
    adj_col = lax.dynamic_slice(adjoint, (low, start), (low, w))
    fac_col = lax.dynamic_slice(factor, (low, start), (low, w))
    cut = w // 2
    top = jnp.concatenate([adj_col, fac_col[:cut]], axis=0)
    bottom = jnp.concatenate([fac_col[cut:], adjoint[w:low, left - w : left]], axis=0)
    row_block = lax.dynamic_slice(factor, (jnp.where(p == 0, low, w), 0), (w, left))
    quarter = row_quarters(row_block)
    top, bottom, quarter = lax.optimization_barrier((top, bottom, quarter))
    top, bottom = column_hops(top, bottom)
    own = row_spread(quarter)
    up = lax.ppermute(own, ROW, ring_pairs(1))
    down = lax.ppermute(own, ROW, ring_pairs(-1))
    even_top, odd_top = column_swap(top)
    even_bottom, odd_bottom = column_swap(bottom)
    terms, a0, l1_below = sums(
        even_top, even_bottom, odd_top, odd_bottom, inverse[0], factor
    )
    across_first = lax.ppermute(up[0], ROW, ring_pairs(1))
    across_second = lax.ppermute(down[1], ROW, ring_pairs(-1))
    terms, across_first, across_second = lax.optimization_barrier((terms, across_first, across_second))
    terms = lax.all_to_all(terms, ROW, 0, 0)
    diag_t, inverse_t, base = invert(inverse, adjoint, a0)

    r31, r_high, r_low = gather_rows(own, down, up, across_first, across_second)
    last = lax.axis_size(COL) - 1
    near = lax.ppermute(r31, COL, [(last, last - 2)])
    far = lax.ppermute(r31, COL, [(last, 1)])
    across = lax.ppermute(r31, COL, [(last, last - 4)])
    r31 = jnp.where(q == last - 2, near, jnp.where(q == 1, far, jnp.where(q == last - 4, across, r31)))
    r31 = jnp.where(q % 2 == 1, r31, lax.ppermute(r31, COL, [(i, i - 1) for i in range(1, last + 1, 2)]))
    terms, diag_t, inverse_t, base = lax.optimization_barrier((terms, diag_t, inverse_t, base))
    shares, small = middle(terms, r31, inverse[1])
    small = lax.all_to_all(small, ROW, 0, 0)
    base = trail(adjoint, base, a0, l1_below, inverse[1], r31, r_high, r_low)
    small, shares, base = lax.optimization_barrier((small, shares, base))
    shares = lax.all_to_all(shares, ROW, 0, 0)
    count = lax.axis_size(COL)
    before, after, across = (
        lax.ppermute(small, COL, [(i, (i + step) % count) for i in range(count)]) for step in (2, -2, 4)
    )
    theirs = lax.ppermute(
        jnp.stack([small, after, across, before]), COL, [(i, i ^ 1) for i in range(count)]
    )
    base = chain(
        small,
        before,
        after,
        across,
        theirs,
        inverse,
        inverse_t,
        diag_t,
        odd_bottom[low - cut :],
        r31,
        r_high,
        r_low,
        base,
    )
    return final(base, shares)


def solution(mesh):
    return jax.shard_map(
        per_device,
        mesh=mesh,
        in_specs=(P(ROW, COL), P(ROW, COL), P()),
        out_specs=P(ROW, COL),
        check_vma=False,
    )
```

```python
import functools

import jax
import jax.numpy as jnp
from jax import lax
from jax.experimental import pallas as pl
from jax.experimental.pallas import tpu as pltpu
from jax.sharding import PartitionSpec as P

ROW = "row"
COL = "col"
RING = 4
VMEM = pl.BlockSpec(memory_space=pltpu.VMEM)
HBM = pl.BlockSpec(memory_space=pltpu.HBM)


def product(left, right):
    return jnp.dot(left, right, precision=lax.Precision.HIGHEST, preferred_element_type=jnp.float32)


def split(value):
    high = value.astype(jnp.bfloat16)
    return high, (value - high.astype(jnp.float32)).astype(jnp.bfloat16)


def product_split(left, right_high, right_low):
    left_high, left_low = split(left)
    dot = functools.partial(jnp.dot, preferred_element_type=jnp.float32)
    return dot(left_high, right_high) + (dot(left_low, right_high) + dot(left_high, right_low))


def masks(width):
    rows = lax.broadcasted_iota(jnp.int32, (width, width), 0)
    cols = lax.broadcasted_iota(jnp.int32, (width, width), 1)
    return rows > cols, rows == cols


def tril(matrix):
    below, diag = masks(matrix.shape[0])
    return jnp.where(below | diag, matrix, 0.0)


def halved_lower(matrix):
    below, diag = masks(matrix.shape[0])
    return jnp.where(below, matrix, jnp.where(diag, 0.5 * matrix, 0.0))


def params(megabytes):
    return pltpu.CompilerParams(vmem_limit_bytes=megabytes << 20)


def cost(flops, bytes_accessed):
    return pl.CostEstimate(flops=flops, bytes_accessed=bytes_accessed, transcendentals=0)


def in_hbm(value):
    return pltpu.with_memory_space_constraint(value, pltpu.HBM)


def tile_shape(*shape):
    return jax.ShapeDtypeStruct(shape, jnp.float32)


def invert_kernel(tiles, adj, a0, out, out_t, base, power, total, held, sems):
    width = tiles.shape[-1]
    low, left = 2 * width, 4 * width
    q = lax.axis_index(COL)
    half = low // 2
    keep = [(slice(i * half, (i + 1) * half), slice(0, adj.shape[1])) for i in range(2)]
    keep += [(slice(low + i * half, low + (i + 1) * half), slice(left, adj.shape[1])) for i in range(2)]
    stage = [held.at[i, :, slice(0, at[1].stop - at[1].start)] for i, at in enumerate(keep)]
    loads = [pltpu.make_async_copy(adj.at[at], dst, sems.at[i]) for i, (at, dst) in enumerate(zip(keep, stage))]
    stores = [pltpu.make_async_copy(src, base.at[at], sems.at[i + 4]) for i, (at, src) in enumerate(zip(keep, stage))]
    for load in loads:
        load.start()
    below, diag = masks(width)
    scales = []
    for j in range(2):
        tile = tiles[j]
        out_t[j] = tile.T
        only = jnp.where(diag, tile, 0.0)
        power[j] = jnp.where(below, tile / jnp.sum(only, axis=1, keepdims=True), 0.0)
        total[j] = jnp.where(diag, 1.0, 0.0) - power[j]
        scales.append(1.0 / jnp.sum(only, axis=0, keepdims=True))

    for load in loads:
        load.wait()

    @pl.when(q == 0)
    def _():
        for i in range(2):
            held[2 + i, :, :width] = a0[i * half : (i + 1) * half, :]

    for store in stores:
        store.start()

    @pl.loop(0, (width - 1).bit_length() - 1)
    def _(step):
        for j in range(2):
            power[j] = product(power[j], power[j])
        for j in range(2):
            total[j] = total[j] + product(total[j], power[j])

    for j in range(2):
        out[j] = (total[j] * scales[j]).T
    for store in stores:
        store.wait()


def invert(tiles, adjoint, a0):
    w = tiles.shape[-1]
    return pl.pallas_call(
        invert_kernel,
        out_shape=(pltpu.HBM((2, w, w), jnp.float32),) * 2 + (pltpu.HBM(adjoint.shape, jnp.float32),),
        in_specs=[VMEM, HBM, VMEM],
        out_specs=(VMEM,) * 2 + (HBM,),
        scratch_shapes=[pltpu.VMEM((2, w, w), jnp.float32)] * 2
        + [pltpu.VMEM((4, w, adjoint.shape[1]), jnp.float32), pltpu.SemaphoreType.DMA((8,))],
        compiler_params=params(14),
        cost_estimate=cost(28 * 12 * w**3, 1 << 20),
        name="invert",
    )(tiles, in_hbm(adjoint), in_hbm(a0))


def rows_kernel(own, down, up, across_first, across_second, corner, r_high, r_low, held, sems):
    w = corner.shape[0]
    left = own.shape[-1]
    quarter = w // RING
    z = lax.axis_index(ROW) // RING
    sources = [own.at[0], down.at[0], across_first, up.at[0], own.at[1], down.at[1], across_second, up.at[1]]
    fetches = [pltpu.make_async_copy(src, held.at[k], sems.at[k]) for k, src in enumerate(sources)]
    for fetch in fetches:
        fetch.start()
    for k, fetch in enumerate(fetches):
        fetch.wait()
        place = pl.multiple_of(lax.rem(z + k, RING) * quarter, quarter)
        high, low = split(held[k])
        target = pl.ds(k // RING * w + place, quarter)
        r_high[target, :] = high
        r_low[target, :] = low
        if k < RING:
            corner[pl.ds(place, quarter), :] = held[k, :, left - w :]


def gather_rows(*pieces):
    shape = pieces[0].shape
    w, left = shape[1] * RING, shape[2]
    panel = pltpu.HBM((2 * w, left), jnp.bfloat16)
    return pl.pallas_call(
        rows_kernel,
        out_shape=(tile_shape(w, w), panel, panel),
        in_specs=[HBM] * len(pieces),
        out_specs=(VMEM,) * 3,
        scratch_shapes=[
            pltpu.VMEM((2 * RING, shape[1], left), jnp.float32),
            pltpu.SemaphoreType.DMA((2 * RING,)),
        ],
        compiler_params=params(8),
        cost_estimate=cost(1 << 10, 1 << 19),
        name="rows",
    )(*[in_hbm(value) for value in pieces])


def small_rows(w, rows):
    return -(-3 * (w // lax.axis_size(COL) // rows) // 8) * 8


def sums_kernel(even_top, even_bottom, odd_top, odd_bottom, inv0, factor, out, a0_out, l1_out, high, low, small, tall):
    step = pl.program_id(0)
    w = inv0.shape[0]
    rows = lax.axis_size(ROW)
    first = lax.axis_index(ROW) == 0
    per_step = w // (w * 4 // rows)
    cols = 4 * w // rows
    piece = small.shape[1] // rows

    @pl.when(step == 0)
    def _():
        cut = w // 2
        l0, l1 = even_top[: 2 * w], odd_top[: 2 * w]
        c0 = jnp.concatenate([even_top[2 * w :], even_bottom[: 2 * w - cut]], axis=0)
        c1 = jnp.concatenate([odd_top[2 * w :], odd_bottom[: 2 * w - cut]], axis=0)
        skip = first & (lax.broadcasted_iota(jnp.int32, l0.shape, 0) < w)
        a0 = jnp.where(skip, 0.0, product(l0, inv0[...]))
        below = jnp.where(skip, 0.0, l1)
        a0_out[...] = a0
        l1_out[...] = below
        high[:, :w], low[:, :w] = split(a0)
        high[:, w:], low[:, w:] = split(below)
        tall[0] = a0.T
        tall[1] = below.T
        share = w // lax.axis_size(COL)
        mine = pl.ds(pl.multiple_of(lax.axis_index(COL) * share, share), share)
        diag_below = jnp.where(skip, 0.0, c0)
        next_below = jnp.where(skip, 0.0, c1)
        raw_next = jnp.where(first, l1[:w], 0.0)
        tall[2, :, :w] = c1[:w].T
        small[0] = jnp.where(first, even_top[mine, :], 0.0) - product(tall[0, mine, :], diag_below)
        small[1] = jnp.where(first, odd_top[mine, :], 0.0) - product(tall[0, mine, :], next_below)
        small[2] = product(tall[1, mine, :], next_below) - product(tall[2, mine, :w], raw_next)

    part = product_split(factor[...].T, high[...], low[...])
    out[:, :cols, :] = part[:, :w].reshape(per_step, cols, w)
    out[:, cols : 2 * cols, :] = part[:, w:].reshape(per_step, cols, w)
    lines = per_step * piece
    for j in range(3):
        part = small[j, pl.ds(pl.multiple_of(step * lines, lines), lines), :]
        at = 2 * cols + j * piece
        out[:, at : at + piece, :] = part.reshape(per_step, piece, w)
    at = 2 * cols + 3 * piece
    out[:, at:, :] = jnp.zeros((per_step, out.shape[1] - at, w), jnp.float32)


def sums(even_top, even_bottom, odd_top, odd_bottom, inv0, factor):
    w = inv0.shape[0]
    rows = lax.axis_size(ROW)
    share = w // lax.axis_size(COL)
    height = 2 * (4 * w // rows) + small_rows(w, rows)
    const = lambda i: (0, 0)
    whole = lambda value: pl.BlockSpec(value.shape, const, pipeline_mode=pl.Buffered(1))
    return pl.pallas_call(
        sums_kernel,
        grid=(4,),
        out_shape=(pltpu.HBM((rows, height, w), jnp.float32),)
        + (pltpu.HBM((2 * w, w), jnp.float32),) * 2,
        in_specs=[whole(even_top), whole(even_bottom), whole(odd_top), whole(odd_bottom), whole(inv0)]
        + [pl.BlockSpec((2 * w, w), lambda i: (1, i))],
        out_specs=(
            pl.BlockSpec((rows // 4, height, w), lambda i: (i, 0, 0)),
            pl.BlockSpec((2 * w, w), const),
            pl.BlockSpec((2 * w, w), const),
        ),
        scratch_shapes=[
            pltpu.VMEM((2 * w, 2 * w), jnp.bfloat16),
            pltpu.VMEM((2 * w, 2 * w), jnp.bfloat16),
            pltpu.VMEM((3, share, w), jnp.float32),
            pltpu.VMEM((3, w, 2 * w), jnp.float32),
        ],
        compiler_params=params(14),
        cost_estimate=cost(4 << 30, 8 << 20),
        name="sums",
    )(even_top, even_bottom, odd_top, odd_bottom, inv0, in_hbm(factor))


def middle_kernel(terms, r31, inv1, out, out_small, r31_v, inv1_v, out_v, small_v, sems):
    rows, cols = out.shape[:2]
    fetches = [
        pltpu.make_async_copy(r31, r31_v, sems.at[0]),
        pltpu.make_async_copy(inv1, inv1_v, sems.at[1]),
    ]
    for fetch in fetches:
        fetch.start()
    small = terms[0, 2 * cols :, :]
    for i in range(1, rows):
        small = small + terms[i, 2 * cols :, :]
    for i in range(rows):
        small_v[i] = small
    stores = [pltpu.make_async_copy(small_v, out_small, sems.at[2])]
    stores[0].start()
    total = terms[0, : 2 * cols, :]
    for i in range(1, rows):
        total = total + terms[i, : 2 * cols, :]
    top = total[:cols]
    for fetch in fetches:
        fetch.wait()
    out_v[0] = top
    out_v[1] = product(total[cols:] - product(top, r31_v[...]), inv1_v[...])
    stores += [pltpu.make_async_copy(out_v.at[min(i, 1)], out.at[i], sems.at[3 + i]) for i in range(rows)]
    for store in stores[1:]:
        store.start()
    for store in stores:
        store.wait()


def middle(terms, r31, inv1):
    rows, height, w = terms.shape
    small = small_rows(w, rows)
    cols = (height - small) // 2
    return pl.pallas_call(
        middle_kernel,
        out_shape=(pltpu.HBM((rows, cols, w), jnp.float32), pltpu.HBM((rows, small, w), jnp.float32)),
        in_specs=[VMEM, HBM, HBM],
        out_specs=(HBM, HBM),
        scratch_shapes=[
            pltpu.VMEM((w, w), jnp.float32),
            pltpu.VMEM((w, w), jnp.float32),
            pltpu.VMEM((2, cols, w), jnp.float32),
            pltpu.VMEM((rows, small, w), jnp.float32),
            pltpu.SemaphoreType.DMA((3 + rows,)),
        ],
        compiler_params=params(10),
        cost_estimate=cost(1 << 28, 6 << 20),
        name="middle",
    )(terms, in_hbm(r31), in_hbm(inv1))


def trail_kernel(adj, a0, l1, inv1, r31, r_high, r_low, base, out, small):
    w = inv1.shape[0]
    left = 4 * w
    q = lax.axis_index(COL)
    last_q = lax.axis_size(COL) - 1

    @pl.when(pl.program_id(0) == 0)
    def _():
        small[0], small[1] = split(inv1[...])
        small[2], small[3] = split(product(r31[...], inv1[...]))

    first = a0[...]
    second = product_split(l1[...], small[0], small[1]) - product_split(first, small[2], small[3])
    lhs = jnp.concatenate([first, second], axis=1)
    out[...] = adj[...] - product_split(lhs, r_high[...], r_low[...])

    @pl.when(q == last_q)
    def _():
        out[:, left - w :] = second


def trail(adjoint, base, a0, l1, inv1, r31, r_high, r_low):
    rows, cols = adjoint.shape
    w = inv1.shape[0]
    steps = 2
    blk = rows // 2 // steps
    low = lambda i: (i, 0)
    block = lambda i: (steps + i, 0)
    whole = lambda value: pl.BlockSpec(value.shape, lambda i: (0, 0), pipeline_mode=pl.Buffered(1))
    return pl.pallas_call(
        trail_kernel,
        grid=(steps,),
        out_shape=pltpu.HBM(adjoint.shape, jnp.float32),
        in_specs=[
            pl.BlockSpec((blk, 4 * w), block),
            pl.BlockSpec((blk, w), low),
            pl.BlockSpec((blk, w), low),
            whole(inv1),
            whole(r31),
            whole(r_high),
            whole(r_low),
            HBM,
        ],
        out_specs=pl.BlockSpec((blk, 4 * w), block),
        scratch_shapes=[pltpu.VMEM((4, w, w), jnp.bfloat16)],
        input_output_aliases={7: 0},
        compiler_params=params(16),
        cost_estimate=cost(4 << 30, 10 << 20),
        name="trail",
    )(*[in_hbm(value) for value in (adjoint, a0, l1, inv1, r31, r_high, r_low, base)])


def chain_kernel(
    mine, before, after, across, theirs, inverse, inverse_t, diag_t, diag31, r31, r_high, r_low, base, out,
    tiles, lhs, diag, r_high_v, r_low_v, rows_buf, sems
):
    w = inverse.shape[-1]
    rows = mine.shape[0]
    p = lax.axis_index(ROW)
    q = lax.axis_index(COL)
    share = w // lax.axis_size(COL)
    piece = share // rows

    @pl.when((p == 0) | (p == rows - 1))
    def _():
        left = 4 * w
        start = jnp.where(p == 0, 2 * w, w)
        region = (pl.ds(start, w), pl.ds(0, left))
        fetches = [
            pltpu.make_async_copy(r_high, r_high_v, sems.at[0]),
            pltpu.make_async_copy(r_low, r_low_v, sems.at[1]),
            pltpu.make_async_copy(base.at[region], rows_buf, sems.at[2]),
        ]
        for fetch in fetches:
            fetch.start()
        core = lax.rem(q, 2)
        for k, shared in ((0, mine), (1, after), (2, across), (3, before)):
            chip = lax.rem(q // 2 + k, RING)
            for other in range(2):
                at = chip * 2 + (1 - core if other else core)
                target = pl.ds(pl.multiple_of(at * share, share), share)
                for j in range(3):
                    lines = slice(j * piece, (j + 1) * piece)
                    value = theirs[k, :, lines, :] if other else shared[:, lines, :]
                    tiles[j, target, :] = value.reshape(share, w)
        t01, x11 = tiles[1], tiles[2]

        def adjoint_diag(j, dprime):
            inner = halved_lower(product(diag_t[j], tril(dprime)))
            wmat = product(product(inverse_t[j], inner), inverse[j])
            return wmat + wmat.T

        known = r31[...]
        side = product(inverse_t[1], x11 + product(known.T, t01))
        g0 = adjoint_diag(0, tiles[0])
        a132 = product(t01 - product(g0, known), inverse[1])
        for fetch in fetches:
            fetch.wait()

        def update(corner):
            rows_buf[...] = rows_buf[...] - product_split(lhs[...], r_high_v[...], r_low_v[...])

            @pl.when(q == lax.axis_size(COL) - 1)
            def _():
                rows_buf[:, left - w :] = corner

            store = pltpu.make_async_copy(rows_buf, out.at[region], sems.at[3])
            store.start()
            store.wait()

        @pl.when(p == 0)
        def _():
            lhs[:, :w] = g0
            lhs[:, w:] = a132
            update(a132)

            @pl.when(q == 0)
            def _():
                diag[...] = halved_lower(g0)
                store = pltpu.make_async_copy(
                    diag, out.at[pl.ds(2 * w, w), pl.ds(left, w)], sems.at[4]
                )
                store.start()
                store.wait()

        @pl.when(p != 0)
        def _():
            a132_t = a132.T
            g1 = adjoint_diag(1, diag31[...] - side - product(a132_t, known))
            lhs[:, :w] = a132_t
            lhs[:, w:] = g1
            update(halved_lower(g1))


def chain(*operands):
    w = operands[5].shape[-1]
    base = operands[-1]
    panel = pltpu.VMEM((2 * w, 4 * w), jnp.bfloat16)
    return pl.pallas_call(
        chain_kernel,
        out_shape=pltpu.HBM(base.shape, jnp.float32),
        in_specs=[VMEM] * (len(operands) - 3) + [HBM] * 3,
        out_specs=HBM,
        scratch_shapes=[
            pltpu.VMEM((3, w, w), jnp.float32),
            pltpu.VMEM((w, 2 * w), jnp.float32),
            pltpu.VMEM((w, w), jnp.float32),
            panel,
            panel,
            pltpu.VMEM((w, 4 * w), jnp.float32),
            pltpu.SemaphoreType.DMA((5,)),
        ],
        input_output_aliases={len(operands) - 1: 0},
        compiler_params=params(18),
        cost_estimate=cost(1 << 20, 1 << 10),
        name="chain",
    )(*operands[:-3], *[in_hbm(value) for value in operands[-3:]])


def final_kernel(base, got, out, got_v, rows_buf, sems):
    rows, cols, w = got.shape
    left = 4 * w
    p = lax.axis_index(ROW)
    q = lax.axis_index(COL)
    last_q = lax.axis_size(COL) - 1

    @pl.when((p == 0) | (p == rows - 1))
    def _():
        start = jnp.where(p == 0, 2 * w, w)
        region = (pl.ds(start, w), pl.ds(0, left))
        fetches = [
            pltpu.make_async_copy(base.at[region], rows_buf, sems.at[0]),
            pltpu.make_async_copy(got, got_v, sems.at[1]),
        ]
        for fetch in fetches:
            fetch.start()
        for fetch in fetches:
            fetch.wait()
        stores = []
        piece = rows // 4
        for j in range(4):
            at = slice(j * w, (j + 1) * w)
            value = rows_buf[:, at] - got_v[j * piece : (j + 1) * piece].reshape(w, w).T
            if j == 3:
                value = jnp.where(q == last_q, rows_buf[:, at], value)
            rows_buf[:, at] = value
            stores.append(
                pltpu.make_async_copy(rows_buf.at[:, at], out.at[pl.ds(start, w), at], sems.at[2 + j])
            )
            stores[-1].start()
        for store in stores:
            store.wait()


def final(base, got):
    w = got.shape[2]
    return pl.pallas_call(
        final_kernel,
        out_shape=tile_shape(*base.shape),
        in_specs=[HBM] * 2,
        out_specs=HBM,
        scratch_shapes=[
            pltpu.VMEM(got.shape, jnp.float32),
            pltpu.VMEM((w, 4 * w), jnp.float32),
            pltpu.SemaphoreType.DMA((6,)),
        ],
        input_output_aliases={0: 0},
        compiler_params=params(8),
        cost_estimate=cost(1 << 20, 4 << 20),
        name="final",
    )(in_hbm(base), in_hbm(got))


def column_hops(top, bottom):
    q = lax.axis_index(COL)
    last = lax.axis_size(COL) - 1
    near, far = [(0, 2), (last, last - 2)], [(0, last - 1), (last, 1)]
    near_top = lax.ppermute(top, COL, near)
    far_bottom = lax.ppermute(bottom, COL, far)
    near_bottom = lax.ppermute(bottom, COL, near)
    far_top = lax.ppermute(top, COL, far)
    upper = lax.ppermute(near_top, COL, [(2, 4), (last - 2, last - 4)])
    lower = lax.ppermute(far_bottom, COL, [(last - 1, 4), (1, last - 4)])

    def choose(own, near_value, far_value, across):
        value = jnp.where((q == 1) | (q == last - 1), far_value, across)
        value = jnp.where((q == 2) | (q == last - 2), near_value, value)
        return jnp.where((q == 0) | (q == last), own, value)

    return choose(top, near_top, far_top, upper), choose(bottom, near_bottom, far_bottom, lower)


def column_swap(mine):
    theirs = lax.ppermute(mine, COL, [(i, i ^ 1) for i in range(lax.axis_size(COL))])
    even = lax.axis_index(COL) % 2 == 0
    return jnp.where(even, mine, theirs), jnp.where(even, theirs, mine)


def row_quarters(block):
    p = lax.axis_index(ROW)
    last = lax.axis_size(ROW) - 1
    top = RING - 1
    quarters = block.reshape(RING, -1, block.shape[1])
    first = p == 0
    near = lax.ppermute(
        jnp.where(first, quarters[1], quarters[top - 1]), ROW, [(0, RING), (last, last - RING)]
    )
    far = lax.ppermute(jnp.where(first, quarters[top], quarters[0]), ROW, [(0, last - top), (last, top)])
    across = lax.ppermute(
        jnp.where(first, quarters[2], quarters[1]), ROW, [(0, 2 * RING), (last, last - 2 * RING)]
    )
    mine = jnp.where(first, quarters[0], quarters[top])
    mine = jnp.where((p == RING) | (p == last - RING), near, mine)
    mine = jnp.where((p == last - top) | (p == top), far, mine)
    return jnp.where((p == 2 * RING) | (p == last - 2 * RING), across, mine)


def row_spread(mine):
    top = RING - 1
    x = lax.axis_index(ROW) % RING
    lines = range(0, lax.axis_size(ROW), RING)
    near = lax.ppermute(mine, ROW, [e for s in lines for e in ((s, s + 1), (s + top, s + top - 1))])
    far = lax.ppermute(mine, ROW, [e for s in lines for e in ((s, s + top), (s + top, s))])
    across = lax.ppermute(mine, ROW, [e for s in lines for e in ((s, s + 2), (s + top, s + top - 2))])
    from_first = jnp.where(x == 0, mine, jnp.where(x == 1, near, jnp.where(x == 2, across, far)))
    from_last = jnp.where(x == top, mine, jnp.where(x == 2, near, jnp.where(x == 1, across, far)))
    return jnp.stack([from_first, from_last])


def ring_pairs(step):
    count = lax.axis_size(ROW)
    return [(i, (i + step * RING) % count) for i in range(count)]


def per_device(factor, adjoint, inverse):
    w = inverse.shape[-1]
    rows = lax.axis_size(ROW)
    p = lax.axis_index(ROW)
    q = lax.axis_index(COL)
    low, left = 2 * w, 4 * w

    start = jnp.where(q == 0, left, left - w)
    adj_col = lax.dynamic_slice(adjoint, (low, start), (low, w))
    fac_col = lax.dynamic_slice(factor, (low, start), (low, w))
    cut = w // 2
    top = jnp.concatenate([adj_col, fac_col[:cut]], axis=0)
    bottom = jnp.concatenate([fac_col[cut:], adjoint[w:low, left - w : left]], axis=0)
    row_block = lax.dynamic_slice(factor, (jnp.where(p == 0, low, w), 0), (w, left))
    quarter = row_quarters(row_block)
    top, quarter = lax.optimization_barrier((top, quarter))
    top, bottom = column_hops(top, bottom)
    own = row_spread(quarter)
    up = lax.ppermute(own, ROW, ring_pairs(1))
    down = lax.ppermute(own, ROW, ring_pairs(-1))
    even_top, odd_top = column_swap(top)
    even_bottom, odd_bottom = column_swap(bottom)
    terms, a0, l1_below = sums(
        even_top, even_bottom, odd_top, odd_bottom, inverse[0], factor
    )
    across_first = lax.ppermute(up[0], ROW, ring_pairs(1))
    across_second = lax.ppermute(down[1], ROW, ring_pairs(-1))
    terms, across_first, across_second = lax.optimization_barrier((terms, across_first, across_second))
    terms = lax.all_to_all(terms, ROW, 0, 0)
    diag_t, inverse_t, base = invert(inverse, adjoint, a0)

    r31, r_high, r_low = gather_rows(own, down, up, across_first, across_second)
    last = lax.axis_size(COL) - 1
    near = lax.ppermute(r31, COL, [(last, last - 2)])
    far = lax.ppermute(r31, COL, [(last, 1)])
    across = lax.ppermute(r31, COL, [(last, last - 4)])
    r31 = jnp.where(q == last - 2, near, jnp.where(q == 1, far, jnp.where(q == last - 4, across, r31)))
    r31 = jnp.where(q % 2 == 1, r31, lax.ppermute(r31, COL, [(i, i - 1) for i in range(1, last + 1, 2)]))
    terms, diag_t, inverse_t, base = lax.optimization_barrier((terms, diag_t, inverse_t, base))
    shares, small = middle(terms, r31, inverse[1])
    small = lax.all_to_all(small, ROW, 0, 0)
    base = trail(adjoint, base, a0, l1_below, inverse[1], r31, r_high, r_low)
    small, shares, base = lax.optimization_barrier((small, shares, base))
    shares = lax.all_to_all(shares, ROW, 0, 0)
    count = lax.axis_size(COL)
    before, after, across = (
        lax.ppermute(small, COL, [(i, (i + step) % count) for i in range(count)]) for step in (2, -2, 4)
    )
    theirs = lax.ppermute(
        jnp.stack([small, after, across, before]), COL, [(i, i ^ 1) for i in range(count)]
    )
    base = chain(
        small,
        before,
        after,
        across,
        theirs,
        inverse,
        inverse_t,
        diag_t,
        odd_bottom[low - cut :],
        r31,
        r_high,
        r_low,
        base,
    )
    return final(base, shares)


def solution(mesh):
    return jax.shard_map(
        per_device,
        mesh=mesh,
        in_specs=(P(ROW, COL), P(ROW, COL), P()),
        out_specs=P(ROW, COL),
        check_vma=False,
    )
```
